512 devices in a mesh: layer: 32 (over x, z_lo, core), lat: 16 (over z_hi, y).
Axes of the slice: x: 4, y: 8, z: 8 (z_hi: 2, z_lo: 4; z = z_hi * 4 + z_lo), core: 2. Of those that a mesh axis runs over, the one named last changes fastest.
Arguments:
- inputs: bfloat16 [4, 128, 2048], P(None, None, 'lat'), may hold values from -6 to 6
- targets: bfloat16 [512, 2048], P(('layer', 'lat')), may hold values from -6 to 6
- top_index: int32 [4, 128, 64], replicated, may hold values from 0 to 8191, all different within a row
- enc_weight: bfloat16 [2048, 32768], P(None, ('layer', 'lat')), may hold values from -0.125 to 0.125
- dec_weight: bfloat16 [32768, 4, 2048], P(('layer', 'lat')), may hold values from -0.375 to 0.375
Outputs:
- errors: float32 [512, 2048], P(('layer', 'lat'))
- grad_enc: bfloat16 [2048, 32768], P(None, ('layer', 'lat'))
- grad_dec: bfloat16 [32768, 4, 2048], P(('layer', 'lat'))
The draws below stay inside these ranges and needn't reach their ends.
Inputs may be any that keep to these rules, and one draw needn't show every extreme that they name: `top_index`: each row names 64 different latents.
All inputs are finite; a program needn't handle non-finite values.
Results may differ from the reference program's by a relative error of at most 0.009.
Values may be sent and summed in bfloat16 or wider, within the bound.
No kernel may reach another device: no remote copies, remote signals or barrier semaphores. Data moves between devices by JAX's collectives and lax.ppermute only.
A program may use at most 64 MiB of HBM per device.

```python
import jax
import jax.numpy as jnp
from jax import lax

D = 2048
F = 8192
K = 64
LAYERS = 4
TOK = 128


def block_levels(rng, extent, split, smallest, top_value):
    def one(position, blocks):
        steps = jax.random.uniform(jax.random.fold_in(jax.random.fold_in(rng, 6), position), (blocks,), jnp.float32, smallest / len(split), top_value / len(split))
        return jnp.repeat(jnp.exp(steps), extent[position] // blocks).reshape((-1,) + (1,) * (len(extent) - position - 1))

    gain = one(*split[0])
    for cut in split[1:]:
        gain = gain * one(*cut)
    return gain


def different_ones(key, rows, amount, top, lift):
    sequence = jax.random.permutation(jax.random.fold_in(key, 1), amount)
    pull = sequence
    for power in range(3):
        pull = pull * pull // amount
    pull = pull * lift // amount
    chance = jax.random.randint(jax.random.fold_in(key, 2), (rows, amount), 0, 4096) + pull
    holders = jax.random.permutation(jax.random.fold_in(key, 3), rows)[jnp.arange(amount) % rows]
    chance = jnp.where(jnp.arange(rows)[:, None] == holders[None, :], 1 << 14, chance)
    score = chance * amount + jnp.arange(amount)
    return lax.top_k(score.astype(jnp.int32), top)[1].astype(jnp.int32)


def normal_values(key, dims, deviation, limit, shards=(), kind=jnp.bfloat16):
    gain = block_levels(key, dims, shards, -0.22, 0.18) if shards else 1.0
    values = jax.random.normal(key, dims, jnp.float32) * deviation * gain
    return jnp.minimum(jnp.maximum(values, -limit), limit).astype(kind)


def setup_inputs(seed: int = 0) -> dict:
    keys = jax.random.split(jax.random.key(seed), 6)
    inputs = normal_values(keys[0], (LAYERS, TOK, D), 1.0, 6.0, ((2, 16),))
    targets = normal_values(keys[1], (LAYERS * TOK, D), 1.0, 6.0, ((0, 512),))
    top_index = different_ones(keys[2], LAYERS * TOK, F, K, 0).reshape((LAYERS, TOK, K))
    enc_weight = normal_values(keys[3], (D, LAYERS * F), D ** -0.5, 0.125, ((1, 512),))
    dec_weight = normal_values(keys[4], (LAYERS * F, LAYERS, D), (K * LAYERS) ** -0.5, 0.375, ((0, 512),))
    return dict(inputs=inputs, targets=targets, top_index=top_index, enc_weight=enc_weight, dec_weight=dec_weight)


def reference(inputs, targets, top_index, enc_weight, dec_weight):
    code_list = []
    active_list = []
    for source in range(LAYERS):
        preact = jnp.dot(inputs[source], enc_weight[:, source * F:(source + 1) * F], preferred_element_type=jnp.float32)
        token_ids = jnp.arange(TOK, dtype=jnp.int32)[:, None]
        active = jnp.zeros((TOK, F), jnp.float32).at[token_ids, top_index[source]].set(1.0)
        active_list.append(active)
        code_list.append((preact * active).astype(jnp.bfloat16))
    decoded_list = []
    for target in range(LAYERS):
        total = jnp.zeros((TOK, D), jnp.float32)
        for source in range(target + 1):
            total = total + jnp.dot(code_list[source], dec_weight[source * F:(source + 1) * F, target, :], preferred_element_type=jnp.float32)
        decoded_list.append(total)
    errors = jnp.concatenate(decoded_list, axis=0) - targets.astype(jnp.float32)
    err_b = errors.astype(jnp.bfloat16).reshape(LAYERS, TOK, D)
    enc_cols = []
    dec_rows = []
    for source in range(LAYERS):
        block = dec_weight[source * F:(source + 1) * F]
        code_grad = jnp.zeros((TOK, F), jnp.float32)
        per_target = []
        for target in range(LAYERS):
            if target >= source:
                code_grad = code_grad + jnp.dot(err_b[target], block[:, target, :].T, preferred_element_type=jnp.float32)
                per_target.append(jnp.dot(code_list[source].T, err_b[target], preferred_element_type=jnp.float32))
            else:
                per_target.append(jnp.zeros((F, D), jnp.float32))
        pre_grad = (code_grad * active_list[source]).astype(jnp.bfloat16)
        enc_cols.append(jnp.dot(inputs[source].T, pre_grad, preferred_element_type=jnp.float32).astype(jnp.bfloat16))
        dec_rows.append(jnp.stack(per_target, axis=1).astype(jnp.bfloat16))
    return errors, jnp.concatenate(enc_cols, axis=1), jnp.concatenate(dec_rows, axis=0)
```

```python
import jax
import jax.numpy as jnp
from jax import lax
from jax.sharding import Mesh
from jax.sharding import PartitionSpec as P

AXES = ("x", "zl", "core", "zh", "y")
GROUP = ("x", "core")
CHIPS = ("zl", "zh", "y")
LAT = ("zh", "y")
F32 = jnp.float32
BF16 = jnp.bfloat16


def exchange(value, axes):
    return lax.all_to_all(value, axes, 0, 0, tiled=True)


def spread(value, axes):
    count = lax.axis_size(axes)
    return exchange(jnp.broadcast_to(value[None], (count,) + value.shape), axes)


def per_device(inputs, targets, top_index, enc_weight, dec_weight):
    layers, tokens, _ = inputs.shape
    lat_dev = enc_weight.shape[1]
    width = dec_weight.shape[2]
    n_x, n_zl, n_core = lax.axis_size("x"), lax.axis_size("zl"), lax.axis_size("core")
    n_lat = lax.axis_size(LAT)
    n_group, n_chips = lax.axis_size(GROUP), lax.axis_size(CHIPS)
    cols = width // n_group
    layer_id = lax.axis_index("x")

    weights = dec_weight.reshape(lat_dev, layers, n_group, cols).transpose(2, 0, 1, 3)
    weights = exchange(weights, GROUP).reshape(n_x, n_core * lat_dev, layers, cols)
    target = exchange(targets.reshape(n_group, 1, cols), GROUP).reshape(layers * n_core, cols)

    own = lax.dynamic_index_in_dim(inputs, layer_id, 0, keepdims=False).T
    features = spread(own, LAT).reshape(width, tokens)
    preact = lax.dot_general(
        enc_weight, features, (((0,), (0,)), ((), ())), preferred_element_type=F32
    )
    chosen = lax.dynamic_index_in_dim(top_index, layer_id, 0, keepdims=False).T
    lat_first = lax.axis_index(("zl", "core", "zh", "y")) * lat_dev
    lat_ids = lat_first + jnp.arange(lat_dev, dtype=jnp.int32)
    active = jnp.any(chosen[None] == lat_ids[:, None, None], axis=1).astype(F32)
    own_codes = (preact * active).astype(BF16)
    codes = spread(own_codes, GROUP).reshape(n_x, n_core * lat_dev, tokens)

    partial = []
    for t in range(layers):
        partial.append(
            lax.dot_general(
                codes[: t + 1].reshape(-1, tokens),
                weights[: t + 1, :, t].reshape(-1, cols),
                (((0,), (0,)), ((), ())),
                preferred_element_type=F32,
            ).astype(BF16)
        )
    partial = jnp.stack(partial).reshape(layers, n_zl, n_core, n_lat, cols)
    partial = partial.transpose(1, 3, 0, 2, 4).reshape(n_chips, layers * n_core, cols)
    partial = exchange(partial, CHIPS)
    errors = jnp.sum(partial.astype(F32), axis=0) - target.astype(F32)
    err_b = spread(errors.astype(BF16), CHIPS)
    err_b = err_b.reshape(n_zl, n_lat, layers, n_core, cols).transpose(2, 0, 3, 1, 4)
    err_b = err_b.reshape(layers, tokens, cols)

    grads, dec_rows = [], []
    for s in range(layers):
        total = jnp.zeros((n_core * lat_dev, tokens), F32)
        rows = []
        for t in range(layers):
            if t < s:
                rows.append(jnp.zeros((n_core * lat_dev, cols), BF16))
                continue
            total = total + lax.dot_general(
                weights[s, :, t], err_b[t], (((1,), (1,)), ((), ())), preferred_element_type=F32
            )
            rows.append(jnp.dot(codes[s], err_b[t], preferred_element_type=F32).astype(BF16))
        grads.append(total)
        dec_rows.append(jnp.stack(rows, axis=1))
    code_grad = jnp.stack(grads).reshape(n_group, lat_dev, tokens)
    code_grad = jnp.sum(exchange(code_grad, GROUP), axis=0)
    dec_rows = jnp.stack(dec_rows).reshape(n_group, lat_dev, layers, cols)
    grad_dec = exchange(dec_rows, GROUP).transpose(1, 2, 0, 3).reshape(lat_dev, layers, width)
    errors = exchange(errors.reshape(n_group, 1, cols), GROUP).reshape(1, width)
    pre_grad = (code_grad * active).astype(BF16)
    grad_enc = lax.dot_general(
        features, pre_grad, (((1,), (1,)), ((), ())), preferred_element_type=F32
    ).astype(BF16)
    return errors, grad_enc, grad_dec


def solution(mesh):
    fine = Mesh(mesh.devices.reshape(4, 4, 2, 2, 8), AXES)
    in_specs = (
        P(None, None, LAT),
        P(AXES, None),
        P(),
        P(None, AXES),
        P(AXES, None, None),
    )
    out_specs = (P(AXES, None), P(None, AXES), P(AXES, None, None))
    return jax.shard_map(
        per_device, mesh=fine, in_specs=in_specs, out_specs=out_specs, check_vma=False
    )
```

```python
import functools

import jax
import jax.numpy as jnp
from jax import lax
from jax.experimental import pallas as pl
from jax.experimental.pallas import tpu as pltpu
from jax.sharding import Mesh
from jax.sharding import PartitionSpec as P

AXES = ("x", "zp", "zn", "core", "zh", "y")
GROUP = ("x", "zn", "core")
CHIPS = ("zp", "zh", "y")
LAT = ("zh", "y")
F32 = jnp.float32
BF16 = jnp.bfloat16


def exchange(value, axes):
    return lax.all_to_all(value, axes, 0, 0, tiled=True)


def dot(a, b, dim_a, dim_b):
    return lax.dot_general(a, b, (((dim_a,), (dim_b,)), ((), ())), preferred_element_type=F32)


def call(body, out_shape, *args, scalars=0, scratch=()):
    specs = [pl.BlockSpec(memory_space=pltpu.SMEM)] * scalars
    specs += [pl.BlockSpec(memory_space=pltpu.VMEM)] * (len(args) - scalars)
    return pl.pallas_call(
        body,
        out_shape=out_shape,
        in_specs=specs,
        out_specs=jax.tree.map(lambda _: pl.BlockSpec(memory_space=pltpu.VMEM), out_shape),
        scratch_shapes=list(scratch),
        compiler_params=pltpu.CompilerParams(vmem_limit_bytes=40 * 1024 * 1024),
    )(*args)


def shape(dims, dtype=BF16):
    return jax.ShapeDtypeStruct(dims, dtype)


def own_slice(place, inputs_ref, out_ref):
    own = inputs_ref[place[0]]
    for j in range(out_ref.shape[0]):
        out_ref[j] = own


def encode(place, features_ref, enc_ref, chosen_ref, codes_ref, active_ref):
    parts, tokens, depth = features_ref.shape
    lat_dev = enc_ref.shape[0]
    total = jnp.zeros((lat_dev, tokens), F32)
    for j in range(parts):
        total = total + dot(enc_ref[:, j * depth : (j + 1) * depth], features_ref[j], 1, 1)
    ids = place[1] + lax.broadcasted_iota(jnp.int32, (lat_dev, tokens), 0)
    chosen = chosen_ref[place[0]]
    active = jnp.zeros((lat_dev, tokens), F32)
    for k in range(chosen.shape[0]):
        active = jnp.where(chosen[k : k + 1] == ids, 1.0, active)
    codes = (total * active).astype(BF16)
    active_ref[...] = active
    for g in range(codes_ref.shape[0]):
        codes_ref[g] = codes


def row_blocks(tokens, n_chips, n_near, n_lat):
    for p in range(n_chips // n_lat):
        for n in range(n_near):
            yield (p * n_near + n) * n_lat, p * n_lat, n


def decode(n_lat, layers, codes_ref, weights_ref, out_ref, rows):
    n_group, lat_dev, tokens = codes_ref.shape
    n_chips, n_rows, cols = out_ref.shape
    n_near = n_group // layers
    flipped = []
    for s in range(layers):
        mine = codes_ref[s * n_near : (s + 1) * n_near].reshape(n_near * lat_dev, tokens)
        flipped.append(mine.T)
    for t in range(layers):
        total = jnp.zeros((tokens, cols), F32)
        for s in range(t + 1):
            near = weights_ref[
                s * n_near : (s + 1) * n_near, t * lat_dev : (t + 1) * lat_dev
            ].reshape(n_near * lat_dev, cols)
            total = total + dot(flipped[s], near, 1, 0)
        for first, chip, n in row_blocks(tokens, n_chips, n_near, n_lat):
            start = chip * n_rows + t * n_near + n
            rows[pl.ds(start, n_lat, stride=n_rows), :] = total[first : first + n_lat]
    out_ref[...] = rows[...].reshape(out_ref.shape).astype(BF16)


def sum_rows(partial_ref, weights_ref, err_ref, pair_ref):
    n_chips, n_rows, cols = partial_ref.shape
    first = weights_ref.shape[1] - 8
    total = partial_ref[0].astype(F32)
    for c in range(1, n_chips):
        total = total + partial_ref[c].astype(F32)
    target = jnp.concatenate(
        [weights_ref[g, first : first + 8][:1].astype(F32) for g in range(n_rows)], axis=0
    )
    errors = total - target
    err_b = errors.astype(BF16)
    high = err_b.astype(F32)
    pair_ref[0] = high
    pair_ref[1] = errors - high
    for c in range(n_chips):
        err_ref[c] = err_b


def backward(n_lat, layers, err_ref, codes_ref, weights_ref, pair_ref, out_ref, rows, mixed):
    n_group, lat_dev, tokens = codes_ref.shape
    n_chips, n_rows, cols = err_ref.shape
    n_near = n_group // layers
    near_lat = n_near * lat_dev
    rows[...] = err_ref[...].astype(F32).reshape(n_chips * n_rows, cols)
    err = []
    for t in range(layers):
        pieces = []
        for first, chip, n in row_blocks(tokens, n_chips, n_near, n_lat):
            start = chip * n_rows + t * n_near + n
            pieces.append(rows[pl.ds(start, n_lat, stride=n_rows), :])
        err.append(jnp.concatenate(pieces, axis=0).astype(BF16))
    dec_rows = layers * lat_dev
    for s in range(layers):
        mine = slice(s * n_near, (s + 1) * n_near)
        codes = codes_ref[mine].reshape(near_lat, tokens)
        total = jnp.zeros((near_lat, tokens), F32)
        for t in range(layers):
            if t < s:
                row = jnp.zeros((near_lat, cols), F32)
            else:
                row = dot(codes, err[t], 1, 0)
                near = weights_ref[mine, t * lat_dev : (t + 1) * lat_dev]
                total = total + dot(near.reshape(near_lat, cols), err[t], 1, 1)
            mixed[pl.ds(t, near_lat, stride=layers), :] = row
        out_ref[mine, 0:dec_rows] = mixed[...].reshape(n_near, dec_rows, cols).astype(BF16)
        total = total.reshape(n_near, lat_dev, tokens).astype(BF16)
        out_ref[mine, dec_rows : dec_rows + lat_dev] = total
    for g in range(n_group):
        high = jnp.broadcast_to(pair_ref[0, g : g + 1], (8, cols))
        low = jnp.broadcast_to(pair_ref[1, g : g + 1], (8, cols))
        first = lax.broadcasted_iota(jnp.int32, (8, cols), 0) == 0
        out_ref[g, dec_rows + lat_dev :] = jnp.where(first, high, low).astype(BF16)


def finish(dec_rows, arrived_ref, features_ref, active_ref, enc_ref, errors_ref):
    n_group, n_rows, cols = arrived_ref.shape
    lat_dev = active_ref.shape[0]
    total = arrived_ref[0, dec_rows : dec_rows + lat_dev].astype(F32)
    for g in range(1, n_group):
        total = total + arrived_ref[g, dec_rows : dec_rows + lat_dev].astype(F32)
    pre_grad = (total * active_ref[...]).astype(BF16)
    parts, _, depth = features_ref.shape
    for j in range(parts):
        enc_ref[:, j * depth : (j + 1) * depth] = dot(pre_grad, features_ref[j], 1, 0).astype(BF16)
    for g in range(n_group):
        pair = arrived_ref[g, dec_rows + lat_dev :].astype(F32)
        errors_ref[:, g * cols : (g + 1) * cols] = pair[0:1] + pair[1:2]


def per_device(inputs, targets, top_index, enc_weight, dec_weight):
    layers, tokens, depth = inputs.shape
    lat_dev = enc_weight.shape[1]
    width = dec_weight.shape[2]
    n_group, n_chips, n_lat = lax.axis_size(GROUP), lax.axis_size(CHIPS), lax.axis_size(LAT)
    cols = width // n_group
    dec_rows = layers * lat_dev
    lat_first = lax.axis_index(("zp", "zn", "core", "zh", "y")) * lat_dev
    place = jnp.stack([lax.axis_index("x"), lat_first]).astype(jnp.int32)

    own = call(own_slice, shape((n_lat, tokens, depth)), place, inputs, scalars=1)
    features = exchange(own, LAT)

    weights = dec_weight.reshape(lat_dev, layers, n_group, cols).transpose(2, 1, 0, 3)
    weights = weights.reshape(n_group, dec_rows, cols)
    target = jnp.broadcast_to(targets.reshape(n_group, 1, cols), (n_group, 8, cols))
    weights = jnp.concatenate([weights, target], axis=1)
    features, weights = lax.optimization_barrier((features, weights))
    weights = exchange(weights, GROUP)

    codes, active = call(
        encode,
        (shape((n_group, lat_dev, tokens)), shape((lat_dev, tokens), F32)),
        place,
        features,
        enc_weight.T,
        top_index.transpose(0, 2, 1),
        scalars=1,
    )
    codes, weights = lax.optimization_barrier((codes, weights))
    codes = exchange(codes, GROUP)

    partial = call(
        functools.partial(decode, n_lat, layers),
        shape((n_chips, n_group, cols)),
        codes,
        weights,
        scratch=[pltpu.VMEM((n_chips * n_group, cols), F32)],
    )
    partial = exchange(partial, CHIPS)
    err_b, pair = call(
        sum_rows,
        (shape((n_chips, n_group, cols)), shape((2, n_group, cols), F32)),
        partial,
        weights,
    )
    err_b = exchange(err_b, CHIPS)
    outgoing = call(
        functools.partial(backward, n_lat, layers),
        shape((n_group, dec_rows + lat_dev + 8, cols)),
        err_b,
        codes,
        weights,
        pair,
        scratch=[
            pltpu.VMEM((n_chips * n_group, cols), F32),
            pltpu.VMEM((n_group * lat_dev, cols), F32),
        ],
    )
    arrived = exchange(outgoing, GROUP)
    grad_enc, errors = call(
        functools.partial(finish, dec_rows),
        (shape((lat_dev, width)), shape((1, width), F32)),
        arrived,
        features,
        active,
    )
    grad_dec = arrived[:, :dec_rows].reshape(n_group, lat_dev, layers, cols)
    grad_dec = grad_dec.transpose(1, 2, 0, 3).reshape(lat_dev, layers, width)
    return errors, grad_enc.T, grad_dec


def solution(mesh):
    fine = Mesh(mesh.devices.reshape(4, 2, 2, 2, 2, 8), AXES)
    in_specs = (
        P(None, None, LAT),
        P(AXES, None),
        P(),
        P(None, AXES),
        P(AXES, None, None),
    )
    out_specs = (P(AXES, None), P(None, AXES), P(AXES, None, None))
    return jax.shard_map(
        per_device, mesh=fine, in_specs=in_specs, out_specs=out_specs, check_vma=False
    )
```

```python
import functools

import jax
import jax.numpy as jnp
from jax import lax
from jax.experimental import pallas as pl
from jax.experimental.pallas import tpu as pltpu
from jax.sharding import Mesh
from jax.sharding import PartitionSpec as P

AXES = ("x", "zp", "zn", "core", "zh", "y")
GROUP = ("x", "core")
CHIPS = ("zp", "zn", "zh", "y")
LAT = ("zh", "y")
NEAR_HALVES = ("zp", "zh", "y")
F32 = jnp.float32
BF16 = jnp.bfloat16
LANES = 128


def exchange(value, axes):
    return lax.all_to_all(value, axes, 0, 0, tiled=True)


def dot(a, b, dim_a, dim_b):
    return lax.dot_general(a, b, (((dim_a,), (dim_b,)), ((), ())), preferred_element_type=F32)


def call(body, out_shape, *args, scalars=0, scratch=()):
    specs = [pl.BlockSpec(memory_space=pltpu.SMEM)] * scalars
    specs += [pl.BlockSpec(memory_space=pltpu.VMEM)] * (len(args) - scalars)
    return pl.pallas_call(
        body,
        out_shape=out_shape,
        in_specs=specs,
        out_specs=jax.tree.map(lambda _: pl.BlockSpec(memory_space=pltpu.VMEM), out_shape),
        scratch_shapes=list(scratch),
        compiler_params=pltpu.CompilerParams(vmem_limit_bytes=40 * 1024 * 1024),
    )(*args)


def shape(dims, dtype=BF16):
    return jax.ShapeDtypeStruct(dims, dtype)


def own_slice(place, inputs_ref, out_ref):
    own = inputs_ref[place[0]]
    for j in range(out_ref.shape[0]):
        out_ref[j] = own


def encode(place, features_ref, enc_ref, chosen_ref, codes_ref, active_ref):
    parts, tokens, depth = features_ref.shape
    lat_dev = enc_ref.shape[0]
    total = jnp.zeros((lat_dev, tokens), F32)
    for j in range(parts):
        total = total + dot(enc_ref[:, j * depth : (j + 1) * depth], features_ref[j], 1, 1)
    ids = place[1] + lax.broadcasted_iota(jnp.int32, (lat_dev, tokens), 0)
    chosen = chosen_ref[place[0]]
    active = jnp.zeros((lat_dev, tokens), F32)
    for k in range(chosen.shape[0]):
        active = jnp.where(chosen[k : k + 1] == ids, 1.0, active)
    codes = (total * active).astype(BF16)
    active_ref[...] = active
    for g in range(codes_ref.shape[0]):
        codes_ref[g] = codes


def row_blocks(tokens, n_chips, n_near, n_lat):
    for p in range(n_chips // n_lat):
        for n in range(n_near):
            yield (p * n_near + n) * n_lat, p * n_lat, n


def decode(n_lat, place, codes_ref, p0, p1, p2, p3, out_ref, weights_ref, *rows):
    n_group, lat_dev, tokens = codes_ref.shape
    n_chips, n_rows, cols = out_ref.shape
    layers = weights_ref.shape[0]
    n_near = n_group // layers
    for d, piece in enumerate((p0, p1, p2, p3)):
        weights_ref[lax.rem(place[0] + layers - d, layers)] = piece[...]
    flipped = []
    for s in range(layers):
        mine = codes_ref[s * n_near : (s + 1) * n_near].reshape(n_near * lat_dev, tokens)
        flipped.append(mine.T)
    for t in range(layers):
        total = jnp.zeros((tokens, cols), F32)
        for s in range(t + 1):
            near = weights_ref[s, t, :, :lat_dev].reshape(n_near * lat_dev, cols)
            total = total + dot(flipped[s], near, 1, 0)
        for first, chip, n in row_blocks(tokens, n_chips, n_near, n_lat):
            start = chip * n_rows + t * n_near + n
            for i, row in enumerate(rows):
                piece = total[first : first + n_lat, i * LANES : (i + 1) * LANES]
                row[pl.ds(start, n_lat, stride=n_rows), :] = piece
    for i, row in enumerate(rows):
        piece = row[...].reshape(n_chips, n_rows, LANES).astype(BF16)
        out_ref[:, :, i * LANES : (i + 1) * LANES] = piece


def sum_rows(partial_ref, weights_ref, err_ref, pair_ref):
    n_chips, n_rows, cols = partial_ref.shape
    layers, _, n_near, padded, _ = weights_ref.shape
    total = partial_ref[0].astype(F32)
    for c in range(1, n_chips):
        total = total + partial_ref[c].astype(F32)
    target = jnp.concatenate(
        [
            weights_ref[t, 0, n, padded - 8 :].astype(F32)[:1]
            for t in range(layers)
            for n in range(n_near)
        ],
        axis=0,
    )
    errors = total - target
    err_b = errors.astype(BF16)
    high = err_b.astype(F32)
    pair_ref[0] = high
    pair_ref[1] = errors - high
    for c in range(n_chips):
        err_ref[c] = err_b


def backward(n_lat, layers, err_ref, codes_ref, weights_ref, pair_ref, out_ref, *scratch):
    n_group, lat_dev, tokens = codes_ref.shape
    n_chips, n_rows, cols = err_ref.shape
    n_near = n_group // layers
    near_lat = n_near * lat_dev
    parts = cols // LANES
    rows, mixed = scratch[:parts], scratch[parts:]
    for i, row in enumerate(rows):
        piece = err_ref[:, :, i * LANES : (i + 1) * LANES].astype(F32)
        row[...] = piece.reshape(n_chips * n_rows, LANES)
    err = []
    for t in range(layers):
        pieces = []
        for first, chip, n in row_blocks(tokens, n_chips, n_near, n_lat):
            start = chip * n_rows + t * n_near + n
            piece = [row[pl.ds(start, n_lat, stride=n_rows), :] for row in rows]
            pieces.append(jnp.concatenate(piece, axis=1))
        err.append(jnp.concatenate(pieces, axis=0).astype(BF16))
    dec_rows = layers * lat_dev
    grad_rows = lat_dev * tokens // cols
    for s in range(layers):
        mine = slice(s * n_near, (s + 1) * n_near)
        codes = codes_ref[mine].reshape(near_lat, tokens)
        total = jnp.zeros((near_lat, tokens), F32)
        for t in range(layers):
            if t < s:
                row = jnp.zeros((near_lat, cols), F32)
            else:
                row = dot(codes, err[t], 1, 0)
                near = weights_ref[s, t, :, :lat_dev]
                total = total + dot(near.reshape(near_lat, cols), err[t], 1, 1)
            for i, part in enumerate(mixed):
                piece = row[:, i * LANES : (i + 1) * LANES]
                part[pl.ds(t, near_lat, stride=layers), :] = piece
        for i, part in enumerate(mixed):
            piece = part[...].reshape(n_near, dec_rows, LANES).astype(BF16)
            out_ref[mine, 0:dec_rows, i * LANES : (i + 1) * LANES] = piece
        total = total.reshape(n_near, cols // tokens, grad_rows, tokens).astype(BF16)
        for i in range(cols // tokens):
            lanes = slice(i * tokens, (i + 1) * tokens)
            out_ref[mine, dec_rows : dec_rows + grad_rows, lanes] = total[:, i]
    for g in range(n_group):
        high = jnp.broadcast_to(pair_ref[0, g : g + 1], (8, cols))
        low = jnp.broadcast_to(pair_ref[1, g : g + 1], (8, cols))
        first = lax.broadcasted_iota(jnp.int32, (8, cols), 0) == 0
        out_ref[g, dec_rows + grad_rows :] = jnp.where(first, high, low).astype(BF16)


def finish(dec_rows, layers, arrived_ref, features_ref, active_ref, enc_ref, errors_ref):
    n_group, _, cols = arrived_ref.shape
    lat_dev, tokens = active_ref.shape
    grad_rows = lat_dev * tokens // cols
    n_near = n_group // layers
    total = arrived_ref[0, dec_rows : dec_rows + grad_rows].astype(F32)
    for g in range(1, n_group):
        total = total + arrived_ref[g, dec_rows : dec_rows + grad_rows].astype(F32)
    halves = [total[:, i * tokens : (i + 1) * tokens] for i in range(cols // tokens)]
    pre_grad = (jnp.concatenate(halves, axis=0) * active_ref[...]).astype(BF16)
    parts, _, depth = features_ref.shape
    for j in range(parts):
        enc_ref[:, j * depth : (j + 1) * depth] = dot(pre_grad, features_ref[j], 1, 0).astype(BF16)
    for g in range(n_group):
        pair = arrived_ref[g, dec_rows + grad_rows :].astype(F32)
        first = (g % n_near * layers + g // n_near) * cols
        errors_ref[:, first : first + cols] = pair[0:1] + pair[1:2]


def shift(value, axis, by):
    count = lax.axis_size(axis)
    return lax.ppermute(value, axis, [(i, (i + by) % count) for i in range(count)])


def per_device(inputs, targets, top_index, enc_weight, dec_weight):
    layers, tokens, depth = inputs.shape
    lat_dev = enc_weight.shape[1]
    width = dec_weight.shape[2]
    n_group, n_chips, n_lat = lax.axis_size(GROUP), lax.axis_size(CHIPS), lax.axis_size(LAT)
    n_near = n_group // layers
    cols = width // n_group
    half = width // n_near
    dec_rows = layers * lat_dev
    grad_rows = lat_dev * tokens // cols
    x, core = lax.axis_index("x"), lax.axis_index("core")
    lat_first = lax.axis_index(("zp", "zn", "core", "zh", "y")) * lat_dev
    place = jnp.stack([x, lat_first]).astype(jnp.int32)

    padded = lat_dev + 8
    target = jnp.broadcast_to(targets[None], (8, layers, width))
    both = jnp.concatenate([dec_weight, target], axis=0)
    kept = lax.dynamic_slice_in_dim(both, core * half, half, 2)
    sent = lax.dynamic_slice_in_dim(both, (1 - core) * half, half, 2)
    came = shift(sent, "core", 1)

    n_y = lax.axis_size("y")
    pairs = [[zp * 2 + 0, (1 - zp) * 2 + 1] for zp in range(2)]
    groups = [[i * n_y + y for i in pair for y in range(n_y)] for pair in pairs]
    own = call(own_slice, shape((n_lat, tokens, depth)), place, inputs, scalars=1)
    features = lax.all_to_all(own, NEAR_HALVES, 0, 0, tiled=True, axis_index_groups=groups)

    mine = jnp.where(core == 0, jnp.stack([kept, came]), jnp.stack([came, kept]))
    mine = mine.reshape(n_near, padded, layers, layers, cols).transpose(3, 2, 0, 1, 4)
    pieces = [lax.dynamic_index_in_dim(mine, x, 0, keepdims=False)]
    for d in range(1, layers):
        piece = lax.dynamic_index_in_dim(mine, (x + d) % layers, 0, keepdims=False)
        pieces.append(shift(piece, "x", d))

    codes, active = call(
        encode,
        (shape((n_group, lat_dev, tokens)), shape((lat_dev, tokens), F32)),
        place,
        features,
        enc_weight.T,
        top_index.transpose(0, 2, 1),
        scalars=1,
    )
    codes = exchange(codes, GROUP)

    partial, weights = call(
        functools.partial(decode, n_lat),
        (shape((n_chips, n_group, cols)), shape((layers, layers, n_near, padded, cols))),
        place,
        codes,
        *pieces,
        scalars=1,
        scratch=[pltpu.VMEM((n_chips * n_group, LANES), F32)] * (cols // LANES),
    )
    partial = exchange(partial, CHIPS)
    err_b, pair = call(
        sum_rows,
        (shape((n_chips, n_group, cols)), shape((2, n_group, cols), F32)),
        partial,
        weights,
    )
    err_b = exchange(err_b, CHIPS)
    outgoing = call(
        functools.partial(backward, n_lat, layers),
        shape((n_group, dec_rows + grad_rows + 8, cols)),
        err_b,
        codes,
        weights,
        pair,
        scratch=[pltpu.VMEM((n_chips * n_group, LANES), F32)] * (cols // LANES)
        + [pltpu.VMEM((n_near * dec_rows, LANES), F32)] * (cols // LANES),
    )
    arrived = exchange(outgoing, GROUP)
    grad_enc, errors = call(
        functools.partial(finish, dec_rows, layers),
        (shape((lat_dev, width)), shape((1, width), F32)),
        arrived,
        features,
        active,
    )
    grad_dec = arrived[:, :dec_rows].reshape(layers, n_near, lat_dev, layers, cols)
    grad_dec = grad_dec.transpose(2, 3, 1, 0, 4).reshape(lat_dev, layers, width)
    return errors, grad_enc.T, grad_dec


def solution(mesh):
    fine = Mesh(mesh.devices.reshape(4, 2, 2, 2, 2, 8), AXES)
    in_specs = (
        P(None, None, LAT),
        P(AXES, None),
        P(),
        P(None, AXES),
        P(AXES, None, None),
    )
    out_specs = (P(AXES, None), P(None, AXES), P(AXES, None, None))
    return jax.shard_map(
        per_device, mesh=fine, in_specs=in_specs, out_specs=out_specs, check_vma=False
    )
```

```python
import functools

import jax
import jax.numpy as jnp
from jax import lax
from jax.experimental import pallas as pl
from jax.experimental.pallas import tpu as pltpu
from jax.sharding import Mesh
from jax.sharding import PartitionSpec as P

AXES = ("x", "zp", "zn", "core", "zh", "y")
GROUP = ("x", "core")
CHIPS = ("zp", "zn", "zh", "y")
LAT = ("zh", "y")
NEAR_HALVES = ("zp", "zh", "y")
F32 = jnp.float32
BF16 = jnp.bfloat16
LANES = 128


def exchange(value, axes):
    return lax.all_to_all(value, axes, 0, 0, tiled=True)


def dot(a, b, dim_a, dim_b):
    return lax.dot_general(a, b, (((dim_a,), (dim_b,)), ((), ())), preferred_element_type=F32)


def call(body, out_shape, *args, scalars=0, scratch=()):
    specs = [pl.BlockSpec(memory_space=pltpu.SMEM)] * scalars
    specs += [pl.BlockSpec(memory_space=pltpu.VMEM)] * (len(args) - scalars)
    return pl.pallas_call(
        body,
        out_shape=out_shape,
        in_specs=specs,
        out_specs=jax.tree.map(lambda _: pl.BlockSpec(memory_space=pltpu.VMEM), out_shape),
        scratch_shapes=list(scratch),
        compiler_params=pltpu.CompilerParams(vmem_limit_bytes=40 * 1024 * 1024),
    )(*args)


def shape(dims, dtype=BF16):
    return jax.ShapeDtypeStruct(dims, dtype)


def own_slice(place, inputs_ref, out_ref):
    own = inputs_ref[place[0]]
    for j in range(out_ref.shape[0]):
        out_ref[j] = own


def encode(
    n_near, place, features_ref, target_ref, enc_ref, chosen_ref, codes_ref, active_ref
):
    parts, tokens, depth = features_ref.shape
    lat_dev = enc_ref.shape[0]
    total = jnp.zeros((lat_dev, tokens), F32)
    for j in range(parts):
        total = total + dot(enc_ref[:, j * depth : (j + 1) * depth], features_ref[j], 1, 1)
    ids = place[1] + lax.broadcasted_iota(jnp.int32, (lat_dev, tokens), 0)
    chosen = chosen_ref[place[0]]
    active = jnp.zeros((lat_dev, tokens), F32)
    for k in range(chosen.shape[0]):
        active = jnp.where(chosen[k : k + 1] == ids, 1.0, active)
    codes = (total * active).astype(BF16)
    active_ref[...] = active
    n_group = codes_ref.shape[0]
    cols = target_ref.shape[1] // n_group
    for g in range(n_group):
        codes_ref[g, :lat_dev] = codes
        first = (g % n_near * (n_group // n_near) + g // n_near) * cols
        target = target_ref[:, first : first + cols].astype(F32)
        pair = [target[:, i : i + LANES] for i in range(0, cols, LANES)]
        rows = jnp.concatenate(pair + [jnp.zeros((8 - len(pair), LANES), F32)], axis=0)
        codes_ref[g, lat_dev:] = rows.astype(BF16)


def row_blocks(tokens, n_chips, n_near, n_lat):
    for p in range(n_chips // n_lat):
        for n in range(n_near):
            yield (p * n_near + n) * n_lat, p * n_lat, n


def arrange(place, after, p0, p1, p2, p3, weights_ref):
    del after
    layers = weights_ref.shape[0]
    for d, piece in enumerate((p0, p1, p2, p3)):
        weights_ref[lax.rem(place[0] + layers - d, layers)] = piece[...]


def decode(n_lat, codes_ref, weights_ref, out_ref, *rows):
    n_group, _, tokens = codes_ref.shape
    n_chips, n_rows, cols = out_ref.shape
    layers, _, _, lat_dev, _ = weights_ref.shape
    n_near = n_group // layers
    flipped = []
    for s in range(layers):
        mine = codes_ref[s * n_near : (s + 1) * n_near, :lat_dev].reshape(-1, tokens)
        flipped.append(mine.T)
    for t in range(layers):
        total = jnp.zeros((tokens, cols), F32)
        for s in range(t + 1):
            near = weights_ref[s, t].reshape(n_near * lat_dev, cols)
            total = total + dot(flipped[s], near, 1, 0)
        for first, chip, n in row_blocks(tokens, n_chips, n_near, n_lat):
            start = chip * n_rows + t * n_near + n
            for i, row in enumerate(rows):
                piece = total[first : first + n_lat, i * LANES : (i + 1) * LANES]
                row[pl.ds(start, n_lat, stride=n_rows), :] = piece
    for i, row in enumerate(rows):
        piece = row[...].reshape(n_chips, n_rows, LANES).astype(BF16)
        out_ref[:, :, i * LANES : (i + 1) * LANES] = piece


def sum_rows(partial_ref, codes_ref, err_ref, pair_ref):
    n_chips, n_rows, cols = partial_ref.shape
    total = partial_ref[0].astype(F32)
    for c in range(1, n_chips):
        total = total + partial_ref[c].astype(F32)
    first = codes_ref.shape[1] - 8
    target = []
    for g in range(n_rows):
        rows = codes_ref[g, first:].astype(F32)
        target.append(jnp.concatenate([rows[i : i + 1] for i in range(cols // LANES)], axis=1))
    target = jnp.concatenate(target, axis=0)
    errors = total - target
    err_b = errors.astype(BF16)
    high = err_b.astype(F32)
    pair_ref[0] = high
    pair_ref[1] = errors - high
    for c in range(n_chips):
        err_ref[c] = err_b


def backward(n_lat, err_ref, codes_ref, weights_ref, pair_ref, out_ref, *scratch):
    n_group, _, tokens = codes_ref.shape
    layers, _, _, lat_dev, _ = weights_ref.shape
    n_chips, n_rows, cols = err_ref.shape
    n_near = n_group // layers
    near_lat = n_near * lat_dev
    parts = cols // LANES
    rows, mixed = scratch[:parts], scratch[parts:]
    for i, row in enumerate(rows):
        piece = err_ref[:, :, i * LANES : (i + 1) * LANES].astype(F32)
        row[...] = piece.reshape(n_chips * n_rows, LANES)
    err = []
    for t in range(layers):
        pieces = []
        for first, chip, n in row_blocks(tokens, n_chips, n_near, n_lat):
            start = chip * n_rows + t * n_near + n
            piece = [row[pl.ds(start, n_lat, stride=n_rows), :] for row in rows]
            pieces.append(jnp.concatenate(piece, axis=1))
        err.append(jnp.concatenate(pieces, axis=0).astype(BF16))
    dec_rows = layers * lat_dev
    grad_rows = lat_dev * LANES // cols
    for s in range(layers):
        mine = slice(s * n_near, (s + 1) * n_near)
        codes = codes_ref[mine, :lat_dev].reshape(near_lat, tokens)
        total = jnp.zeros((near_lat, tokens), F32)
        for t in range(layers):
            if t < s:
                row = jnp.zeros((near_lat, cols), F32)
            else:
                row = dot(codes, err[t], 1, 0)
                near = weights_ref[s, t]
                total = total + dot(near.reshape(near_lat, cols), err[t], 1, 1)
            for i, part in enumerate(mixed):
                piece = row[:, i * LANES : (i + 1) * LANES]
                part[pl.ds(t, near_lat, stride=layers), :] = piece
        for i, part in enumerate(mixed):
            piece = part[...].reshape(n_near, dec_rows, LANES).astype(BF16)
            out_ref[mine, i, 0:dec_rows] = piece
        total = total.reshape(n_near, parts, grad_rows, tokens).astype(BF16)
        out_ref[mine, :, dec_rows : dec_rows + grad_rows] = total
    for g in range(n_group):
        for i in range(parts):
            lanes = slice(i * LANES, (i + 1) * LANES)
            high = jnp.broadcast_to(pair_ref[0, g : g + 1, lanes], (8, LANES))
            low = jnp.broadcast_to(pair_ref[1, g : g + 1, lanes], (8, LANES))
            first = lax.broadcasted_iota(jnp.int32, (8, LANES), 0) == 0
            out_ref[g, i, dec_rows + grad_rows :] = jnp.where(first, high, low).astype(BF16)


def finish(
    layers, arrived_ref, tiles_ref, features_ref, active_ref, enc_ref, errors_ref, dec_ref, sem
):
    n_group, parts, n_rows, _ = arrived_ref.shape
    lat_dev, tokens = active_ref.shape
    grad_rows = lat_dev // parts
    dec_rows = n_rows - grad_rows - 8
    n_near = n_group // layers

    def column(g, i):
        return ((g % n_near * layers + g // n_near) * parts + i) * LANES

    copies = []
    for g in range(n_group):
        for i in range(parts):
            copy = pltpu.make_async_copy(
                tiles_ref.at[g, i, 0:lat_dev],
                dec_ref.at[:, :, pl.ds(column(g, i), LANES)],
                sem.at[g * parts + i],
            )
            copy.start()
            copies.append(copy)
    halves = []
    for i in range(parts):
        total = arrived_ref[0, i, dec_rows : dec_rows + grad_rows].astype(F32)
        for g in range(1, n_group):
            total = total + arrived_ref[g, i, dec_rows : dec_rows + grad_rows].astype(F32)
        halves.append(total)
    pre_grad = (jnp.concatenate(halves, axis=0) * active_ref[...]).astype(BF16)
    blocks, _, depth = features_ref.shape
    for j in range(blocks):
        enc_ref[:, j * depth : (j + 1) * depth] = dot(pre_grad, features_ref[j], 1, 0).astype(BF16)
    for g in range(n_group):
        for i in range(parts):
            pair = arrived_ref[g, i, dec_rows + grad_rows :].astype(F32)
            errors_ref[:, column(g, i) : column(g, i) + LANES] = pair[0:1] + pair[1:2]
    for copy in copies:
        copy.wait()


def shift(value, axis, by):
    count = lax.axis_size(axis)
    return lax.ppermute(value, axis, [(i, (i + by) % count) for i in range(count)])


def per_device(inputs, targets, top_index, enc_weight, dec_weight):
    layers, tokens, depth = inputs.shape
    lat_dev = enc_weight.shape[1]
    width = dec_weight.shape[2]
    n_group, n_chips, n_lat = lax.axis_size(GROUP), lax.axis_size(CHIPS), lax.axis_size(LAT)
    n_near = n_group // layers
    cols = width // n_group
    half = width // n_near
    dec_rows = layers * lat_dev
    grad_rows = lat_dev * LANES // cols
    parts = cols // LANES
    x, core = lax.axis_index("x"), lax.axis_index("core")
    lat_first = lax.axis_index(("zp", "zn", "core", "zh", "y")) * lat_dev
    place = jnp.stack([x, lat_first]).astype(jnp.int32)

    n_y = lax.axis_size("y")
    pairs = [[zp * 2 + 0, (1 - zp) * 2 + 1] for zp in range(2)]
    groups = [[i * n_y + y for i in pair for y in range(n_y)] for pair in pairs]
    own = call(own_slice, shape((n_lat, tokens, depth)), place, inputs, scalars=1)
    features = lax.all_to_all(own, NEAR_HALVES, 0, 0, tiled=True, axis_index_groups=groups)

    came = shift(dec_weight, "core", 1)
    kept, came = lax.optimization_barrier((dec_weight, came))
    kept = lax.dynamic_slice_in_dim(kept, core * half, half, 2)
    came = lax.dynamic_slice_in_dim(came, core * half, half, 2)
    mine = jnp.where(core == 0, jnp.stack([kept, came]), jnp.stack([came, kept]))
    mine = mine.reshape(n_near, lat_dev, layers, layers, cols).transpose(3, 2, 0, 1, 4)
    pieces = [lax.dynamic_index_in_dim(mine, x, 0, keepdims=False)]
    for d in range(1, layers):
        piece = lax.dynamic_index_in_dim(mine, (x + d) % layers, 0, keepdims=False)
        pieces.append(shift(piece, "x", d))

    codes, active = call(
        functools.partial(encode, n_near),
        (shape((n_group, lat_dev + 8, tokens)), shape((lat_dev, tokens), F32)),
        place,
        features,
        targets,
        enc_weight.T,
        top_index.transpose(0, 2, 1),
        scalars=1,
    )
    codes = exchange(codes, GROUP)
    weights = call(
        arrange,
        shape((layers, layers, n_near, lat_dev, cols)),
        place,
        active,
        *pieces,
        scalars=1,
    )

    partial = call(
        functools.partial(decode, n_lat),
        shape((n_chips, n_group, cols)),
        codes,
        weights,
        scratch=[pltpu.VMEM((n_chips * n_group, LANES), F32)] * (cols // LANES),
    )
    partial = exchange(partial, CHIPS)
    err_b, pair = call(
        sum_rows,
        (shape((n_chips, n_group, cols)), shape((2, n_group, cols), F32)),
        partial,
        codes,
    )
    err_b = exchange(err_b, CHIPS)
    outgoing = call(
        functools.partial(backward, n_lat),
        shape((n_group, parts, dec_rows + grad_rows + 8, LANES)),
        err_b,
        codes,
        weights,
        pair,
        scratch=[pltpu.VMEM((n_chips * n_group, LANES), F32)] * (cols // LANES)
        + [pltpu.VMEM((n_near * dec_rows, LANES), F32)] * (cols // LANES),
    )
    arrived = exchange(outgoing, GROUP)
    anywhere = pl.BlockSpec(memory_space=pl.ANY)
    vmem = pl.BlockSpec(memory_space=pltpu.VMEM)
    grad_enc, errors, grad_dec = pl.pallas_call(
        functools.partial(finish, layers),
        out_shape=(
            shape((lat_dev, width)),
            shape((1, width), F32),
            shape((lat_dev, layers, width)),
        ),
        in_specs=[vmem, anywhere, vmem, vmem],
        out_specs=(vmem, vmem, anywhere),
        scratch_shapes=[pltpu.SemaphoreType.DMA((n_group * parts,))],
    )(arrived, arrived.reshape(n_group, parts, -1, layers, LANES), features, active)
    return errors, grad_enc.T, grad_dec


def solution(mesh):
    fine = Mesh(mesh.devices.reshape(4, 2, 2, 2, 2, 8), AXES)
    in_specs = (
        P(None, None, LAT),
        P(AXES, None),
        P(),
        P(None, AXES),
        P(AXES, None, None),
    )
    out_specs = (P(AXES, None), P(None, AXES), P(AXES, None, None))
    return jax.shard_map(
        per_device, mesh=fine, in_specs=in_specs, out_specs=out_specs, check_vma=False
    )
```

```python
import functools

import jax
import jax.numpy as jnp
from jax import lax
from jax.experimental import pallas as pl
from jax.experimental.pallas import tpu as pltpu
from jax.sharding import Mesh
from jax.sharding import PartitionSpec as P

AXES = ("x", "zp", "zn", "core", "zh", "y")
GROUP = ("x", "core")
CHIPS = ("zp", "zn", "zh", "y")
LAT = ("zh", "y")
NEAR_HALVES = ("zp", "zh", "y")
F32 = jnp.float32
BF16 = jnp.bfloat16
LANES = 128


def exchange(value, axes):
    return lax.all_to_all(value, axes, 0, 0, tiled=True)


def dot(a, b, dim_a, dim_b):
    return lax.dot_general(a, b, (((dim_a,), (dim_b,)), ((), ())), preferred_element_type=F32)


def call(body, out_shape, *args, scalars=0, scratch=()):
    specs = [pl.BlockSpec(memory_space=pltpu.SMEM)] * scalars
    specs += [pl.BlockSpec(memory_space=pltpu.VMEM)] * (len(args) - scalars)
    return pl.pallas_call(
        body,
        out_shape=out_shape,
        in_specs=specs,
        out_specs=jax.tree.map(lambda _: pl.BlockSpec(memory_space=pltpu.VMEM), out_shape),
        scratch_shapes=list(scratch),
        compiler_params=pltpu.CompilerParams(vmem_limit_bytes=40 * 1024 * 1024),
    )(*args)


def shape(dims, dtype=BF16):
    return jax.ShapeDtypeStruct(dims, dtype)


def own_slice(place, inputs_ref, out_ref, own_ref, sem):
    copy = pltpu.make_async_copy(inputs_ref.at[place[0]], own_ref, sem)
    copy.start()
    copy.wait()
    own = own_ref[...]
    for j in range(out_ref.shape[0]):
        out_ref[j] = own


def find_active(place, chosen_ref, active_ref):
    ids = place[1] + lax.broadcasted_iota(jnp.int32, active_ref.shape, 0)
    chosen = chosen_ref[place[0]]
    active = jnp.zeros(active_ref.shape, F32)
    for k in range(chosen.shape[0]):
        active = jnp.where(chosen[k : k + 1] == ids, 1.0, active)
    active_ref[...] = active


def encode(n_near, features_ref, target_ref, enc_ref, active_ref, codes_ref):
    parts, tokens, depth = features_ref.shape
    lat_dev = enc_ref.shape[0]
    total = jnp.zeros((lat_dev, tokens), F32)
    for j in range(0, parts, 2):
        pair = jnp.concatenate([features_ref[j], features_ref[j + 1]], axis=1)
        total = total + dot(enc_ref[:, j * depth : (j + 2) * depth], pair, 1, 1)
    codes = (total * active_ref[...]).astype(BF16)
    n_group = codes_ref.shape[0]
    cols = target_ref.shape[1] // n_group
    for g in range(n_group):
        codes_ref[g, :lat_dev] = codes
        first = (g % n_near * (n_group // n_near) + g // n_near) * cols
        target = target_ref[:, first : first + cols].astype(F32)
        pair = [target[:, i : i + LANES] for i in range(0, cols, LANES)]
        rows = jnp.concatenate(pair + [jnp.zeros((8 - len(pair), LANES), F32)], axis=0)
        codes_ref[g, lat_dev:] = rows.astype(BF16)


def row_blocks(tokens, n_chips, n_near, n_lat):
    for p in range(n_chips // n_lat):
        for n in range(n_near):
            yield (p * n_near + n) * n_lat, p * n_lat, n


def arrange(place, after, p0, p1, p2, p3, weights_ref):
    del after
    layers = weights_ref.shape[0]
    for d, piece in enumerate((p0, p1, p2, p3)):
        weights_ref[lax.rem(place[0] + layers - d, layers)] = piece[...]


def decode(n_lat, codes_ref, weights_ref, out_ref, *rows):
    n_group, _, tokens = codes_ref.shape
    n_chips, n_rows, cols = out_ref.shape
    layers, _, _, lat_dev, _ = weights_ref.shape
    n_near = n_group // layers
    flipped = []
    for s in range(layers):
        mine = codes_ref[s * n_near : (s + 1) * n_near, :lat_dev].reshape(-1, tokens)
        flipped.append(mine.T)
    for t in range(layers):
        total = jnp.zeros((tokens, cols), F32)
        for s in range(t + 1):
            near = weights_ref[s, t].reshape(n_near * lat_dev, cols)
            total = total + dot(flipped[s], near, 1, 0)
        for first, chip, n in row_blocks(tokens, n_chips, n_near, n_lat):
            start = chip * n_rows + t * n_near + n
            for i, row in enumerate(rows):
                piece = total[first : first + n_lat, i * LANES : (i + 1) * LANES]
                row[pl.ds(start, n_lat, stride=n_rows), :] = piece
    for i, row in enumerate(rows):
        piece = row[...].reshape(n_chips, n_rows, LANES).astype(BF16)
        out_ref[:, :, i * LANES : (i + 1) * LANES] = piece


def sum_rows(partial_ref, codes_ref, err_ref, pair_ref):
    n_chips, n_rows, cols = partial_ref.shape
    total = partial_ref[0].astype(F32)
    for c in range(1, n_chips):
        total = total + partial_ref[c].astype(F32)
    first = codes_ref.shape[1] - 8
    target = []
    for g in range(n_rows):
        rows = codes_ref[g, first:].astype(F32)
        target.append(jnp.concatenate([rows[i : i + 1] for i in range(cols // LANES)], axis=1))
    target = jnp.concatenate(target, axis=0)
    errors = total - target
    err_b = errors.astype(BF16)
    high = err_b.astype(F32)
    pair_ref[0] = high
    pair_ref[1] = errors - high
    for c in range(n_chips):
        err_ref[c] = err_b


def backward(n_lat, err_ref, codes_ref, weights_ref, pair_ref, out_ref, *scratch):
    n_group, _, tokens = codes_ref.shape
    layers, _, _, lat_dev, _ = weights_ref.shape
    n_chips, n_rows, cols = err_ref.shape
    n_near = n_group // layers
    near_lat = n_near * lat_dev
    parts = cols // LANES
    rows, mixed = scratch[:parts], scratch[parts:]
    for i, row in enumerate(rows):
        piece = err_ref[:, :, i * LANES : (i + 1) * LANES].astype(F32)
        row[...] = piece.reshape(n_chips * n_rows, LANES)
    err = []
    for t in range(layers):
        pieces = []
        for first, chip, n in row_blocks(tokens, n_chips, n_near, n_lat):
            start = chip * n_rows + t * n_near + n
            piece = [row[pl.ds(start, n_lat, stride=n_rows), :] for row in rows]
            pieces.append(jnp.concatenate(piece, axis=1))
        err.append(jnp.concatenate(pieces, axis=0).astype(BF16))
    dec_rows = layers * lat_dev
    grad_rows = lat_dev * LANES // cols
    for s in range(layers):
        mine = slice(s * n_near, (s + 1) * n_near)
        codes = codes_ref[mine, :lat_dev].reshape(near_lat, tokens)
        total = jnp.zeros((near_lat, tokens), F32)
        for t in range(layers):
            if t < s:
                row = jnp.zeros((near_lat, cols), F32)
            else:
                row = dot(codes, err[t], 1, 0)
                near = weights_ref[s, t]
                total = total + dot(near.reshape(near_lat, cols), err[t], 1, 1)
            for i, part in enumerate(mixed):
                piece = row[:, i * LANES : (i + 1) * LANES]
                part[pl.ds(t, near_lat, stride=layers), :] = piece
        for i, part in enumerate(mixed):
            piece = part[...].reshape(n_near, dec_rows, LANES).astype(BF16)
            out_ref[mine, i, 0:dec_rows] = piece
        total = total.reshape(n_near, parts, grad_rows, tokens).astype(BF16)
        out_ref[mine, :, dec_rows : dec_rows + grad_rows] = total
    for g in range(n_group):
        for i in range(parts):
            lanes = slice(i * LANES, (i + 1) * LANES)
            high = jnp.broadcast_to(pair_ref[0, g : g + 1, lanes], (8, LANES))
            low = jnp.broadcast_to(pair_ref[1, g : g + 1, lanes], (8, LANES))
            first = lax.broadcasted_iota(jnp.int32, (8, LANES), 0) == 0
            out_ref[g, i, dec_rows + grad_rows :] = jnp.where(first, high, low).astype(BF16)


def finish(
    layers, arrived_ref, tiles_ref, features_ref, active_ref, enc_ref, errors_ref, dec_ref
):
    n_group, parts, n_rows, _ = arrived_ref.shape
    lat_dev, tokens = active_ref.shape
    grad_rows = lat_dev // parts
    dec_rows = n_rows - grad_rows - 8
    n_near = n_group // layers

    def column(g, i):
        return ((g % n_near * layers + g // n_near) * parts + i) * LANES

    for g in range(n_group):
        for i in range(parts):
            first = column(g, i)
            dec_ref[:, :, first : first + LANES] = tiles_ref[g, i, 0:lat_dev]
    halves = []
    for i in range(parts):
        total = arrived_ref[0, i, dec_rows : dec_rows + grad_rows].astype(F32)
        for g in range(1, n_group):
            total = total + arrived_ref[g, i, dec_rows : dec_rows + grad_rows].astype(F32)
        halves.append(total)
    pre_grad = (jnp.concatenate(halves, axis=0) * active_ref[...]).astype(BF16)
    blocks, _, depth = features_ref.shape
    for j in range(blocks):
        enc_ref[:, j * depth : (j + 1) * depth] = dot(pre_grad, features_ref[j], 1, 0).astype(BF16)
    for g in range(n_group):
        for i in range(parts):
            pair = arrived_ref[g, i, dec_rows + grad_rows :].astype(F32)
            errors_ref[:, column(g, i) : column(g, i) + LANES] = pair[0:1] + pair[1:2]


def shift(value, axis, by):
    count = lax.axis_size(axis)
    return lax.ppermute(value, axis, [(i, (i + by) % count) for i in range(count)])


def per_device(inputs, targets, top_index, enc_weight, dec_weight):
    layers, tokens, depth = inputs.shape
    lat_dev = enc_weight.shape[1]
    width = dec_weight.shape[2]
    n_group, n_chips, n_lat = lax.axis_size(GROUP), lax.axis_size(CHIPS), lax.axis_size(LAT)
    n_near = n_group // layers
    cols = width // n_group
    half = width // n_near
    dec_rows = layers * lat_dev
    grad_rows = lat_dev * LANES // cols
    parts = cols // LANES
    x, core = lax.axis_index("x"), lax.axis_index("core")
    lat_first = lax.axis_index(("zp", "zn", "core", "zh", "y")) * lat_dev
    place = jnp.stack([x, lat_first]).astype(jnp.int32)

    n_y = lax.axis_size("y")
    pairs = [[zp * 2 + 0, (1 - zp) * 2 + 1] for zp in range(2)]
    groups = [[i * n_y + y for i in pair for y in range(n_y)] for pair in pairs]
    anywhere = pl.BlockSpec(memory_space=pl.ANY)
    own = pl.pallas_call(
        own_slice,
        out_shape=shape((n_lat, tokens, depth)),
        in_specs=[pl.BlockSpec(memory_space=pltpu.SMEM), anywhere],
        out_specs=pl.BlockSpec(memory_space=pltpu.VMEM),
        scratch_shapes=[pltpu.VMEM((tokens, depth), BF16), pltpu.SemaphoreType.DMA],
    )(place, inputs)
    features = lax.all_to_all(own, NEAR_HALVES, 0, 0, tiled=True, axis_index_groups=groups)

    came = shift(dec_weight, "core", 1)
    kept, came = lax.optimization_barrier((dec_weight, came))
    kept = lax.dynamic_slice_in_dim(kept, core * half, half, 2)
    came = lax.dynamic_slice_in_dim(came, core * half, half, 2)
    mine = jnp.where(core == 0, jnp.stack([kept, came]), jnp.stack([came, kept]))
    mine = mine.reshape(n_near, lat_dev, layers, layers, cols).transpose(3, 2, 0, 1, 4)
    active = call(
        find_active,
        shape((lat_dev, tokens), F32),
        place,
        top_index.transpose(0, 2, 1),
        scalars=1,
    )
    codes = call(
        functools.partial(encode, n_near),
        shape((n_group, lat_dev + 8, tokens)),
        features,
        targets,
        enc_weight.T,
        active,
    )
    pieces = []
    for d in range(layers):
        pieces.append(lax.dynamic_index_in_dim(mine, (x + d) % layers, 0, keepdims=False))

    pieces = [pieces[0]] + [shift(pieces[d], "x", d) for d in range(1, layers)]
    arrived_codes = exchange(codes, GROUP)
    weights = call(
        arrange,
        shape((layers, layers, n_near, lat_dev, cols)),
        place,
        codes,
        *pieces,
        scalars=1,
    )

    partial = call(
        functools.partial(decode, n_lat),
        shape((n_chips, n_group, cols)),
        arrived_codes,
        weights,
        scratch=[pltpu.VMEM((n_chips * n_group, LANES), F32)] * (cols // LANES),
    )
    partial = exchange(partial, CHIPS)
    err_b, pair = call(
        sum_rows,
        (shape((n_chips, n_group, cols)), shape((2, n_group, cols), F32)),
        partial,
        arrived_codes,
    )
    err_b = exchange(err_b, CHIPS)
    outgoing = call(
        functools.partial(backward, n_lat),
        shape((n_group, parts, dec_rows + grad_rows + 8, LANES)),
        err_b,
        arrived_codes,
        weights,
        pair,
        scratch=[pltpu.VMEM((n_chips * n_group, LANES), F32)] * (cols // LANES)
        + [pltpu.VMEM((n_near * dec_rows, LANES), F32)] * (cols // LANES),
    )
    arrived = exchange(outgoing, GROUP)
    grad_enc, errors, grad_dec = call(
        functools.partial(finish, layers),
        (shape((lat_dev, width)), shape((1, width), F32), shape((lat_dev, layers, width))),
        arrived,
        arrived.reshape(n_group, parts, -1, layers, LANES),
        features,
        active,
    )
    return errors, grad_enc.T, grad_dec


def solution(mesh):
    fine = Mesh(mesh.devices.reshape(4, 2, 2, 2, 2, 8), AXES)
    in_specs = (
        P(None, None, LAT),
        P(AXES, None),
        P(),
        P(None, AXES),
        P(AXES, None, None),
    )
    out_specs = (P(AXES, None), P(None, AXES), P(AXES, None, None))
    return jax.shard_map(
        per_device, mesh=fine, in_specs=in_specs, out_specs=out_specs, check_vma=False
    )
```

```python
import functools

import jax
import jax.numpy as jnp
from jax import lax
from jax.experimental import pallas as pl
from jax.experimental.pallas import tpu as pltpu
from jax.sharding import Mesh
from jax.sharding import PartitionSpec as P

AXES = ("x", "zp", "zn", "core", "zh", "y")
GROUP = ("x", "core")
CHIPS = ("zp", "zn", "zh", "y")
LAT = ("zh", "y")
NEAR_HALVES = ("zp", "zh", "y")
F32 = jnp.float32
BF16 = jnp.bfloat16
LANES = 128


def exchange(value, axes):
    return lax.all_to_all(value, axes, 0, 0, tiled=True)


def dot(a, b, dim_a, dim_b):
    return lax.dot_general(a, b, (((dim_a,), (dim_b,)), ((), ())), preferred_element_type=F32)


def call(body, out_shape, *args, scalars=0, scratch=()):
    specs = [pl.BlockSpec(memory_space=pltpu.SMEM)] * scalars
    specs += [pl.BlockSpec(memory_space=pltpu.VMEM)] * (len(args) - scalars)
    return pl.pallas_call(
        body,
        out_shape=out_shape,
        in_specs=specs,
        out_specs=jax.tree.map(lambda _: pl.BlockSpec(memory_space=pltpu.VMEM), out_shape),
        scratch_shapes=list(scratch),
        compiler_params=pltpu.CompilerParams(vmem_limit_bytes=40 * 1024 * 1024),
    )(*args)


def shape(dims, dtype=BF16):
    return jax.ShapeDtypeStruct(dims, dtype)


def find_active(place, chosen_ref, active_ref):
    ids = place[1] + lax.broadcasted_iota(jnp.int32, active_ref.shape, 0)
    chosen = chosen_ref[place[0]]
    active = jnp.zeros(active_ref.shape, F32)
    for k in range(chosen.shape[0]):
        active = jnp.where(chosen[k : k + 1] == ids, 1.0, active)
    active_ref[...] = active


def encode(n_near, features_ref, target_ref, enc_ref, active_ref, codes_ref):
    parts, tokens, depth = features_ref.shape
    lat_dev = enc_ref.shape[0]
    total = jnp.zeros((lat_dev, tokens), F32)
    for j in range(0, parts, 2):
        pair = jnp.concatenate([features_ref[j], features_ref[j + 1]], axis=1)
        total = total + dot(enc_ref[:, j * depth : (j + 2) * depth], pair, 1, 1)
    codes = (total * active_ref[...]).astype(BF16)
    n_group = codes_ref.shape[0]
    cols = target_ref.shape[1] // n_group
    for g in range(n_group):
        codes_ref[g, :lat_dev] = codes
        first = (g % n_near * (n_group // n_near) + g // n_near) * cols
        target = target_ref[:, first : first + cols].astype(F32)
        pair = [target[:, i : i + LANES] for i in range(0, cols, LANES)]
        rows = jnp.concatenate(pair + [jnp.zeros((8 - len(pair), LANES), F32)], axis=0)
        codes_ref[g, lat_dev:] = rows.astype(BF16)


def row_blocks(tokens, n_chips, n_near, n_lat):
    for p in range(n_chips // n_lat):
        for n in range(n_near):
            yield (p * n_near + n) * n_lat, p * n_lat, n


def arrange(order, place, after, p0, p1, p2, p3, weights_ref):
    del after
    layers = weights_ref.shape[0]
    for d, piece in zip(order, (p0, p1, p2, p3)):
        weights_ref[lax.rem(place[0] + layers - d, layers)] = piece[...]


def decode(n_lat, codes_ref, weights_ref, out_ref, *rows):
    n_group, _, tokens = codes_ref.shape
    n_chips, n_rows, cols = out_ref.shape
    layers, _, _, lat_dev, _ = weights_ref.shape
    n_near = n_group // layers
    flipped = []
    for s in range(layers):
        mine = codes_ref[s * n_near : (s + 1) * n_near, :lat_dev].reshape(-1, tokens)
        flipped.append(mine.T)
    for t in range(layers):
        total = jnp.zeros((tokens, cols), F32)
        for s in range(t + 1):
            near = weights_ref[s, t].reshape(n_near * lat_dev, cols)
            total = total + dot(flipped[s], near, 1, 0)
        for first, chip, n in row_blocks(tokens, n_chips, n_near, n_lat):
            start = chip * n_rows + t * n_near + n
            for i, row in enumerate(rows):
                piece = total[first : first + n_lat, i * LANES : (i + 1) * LANES]
                row[pl.ds(start, n_lat, stride=n_rows), :] = piece
    for i, row in enumerate(rows):
        piece = row[...].reshape(n_chips, n_rows, LANES).astype(BF16)
        out_ref[:, :, i * LANES : (i + 1) * LANES] = piece


def sum_rows(partial_ref, codes_ref, err_ref, pair_ref):
    n_chips, n_rows, cols = partial_ref.shape
    total = partial_ref[0].astype(F32)
    for c in range(1, n_chips):
        total = total + partial_ref[c].astype(F32)
    first = codes_ref.shape[1] - 8
    target = []
    for g in range(n_rows):
        rows = codes_ref[g, first:].astype(F32)
        target.append(jnp.concatenate([rows[i : i + 1] for i in range(cols // LANES)], axis=1))
    target = jnp.concatenate(target, axis=0)
    errors = total - target
    err_b = errors.astype(BF16)
    high = err_b.astype(F32)
    pair_ref[0] = high
    pair_ref[1] = errors - high
    for c in range(n_chips):
        err_ref[c] = err_b


def backward(n_lat, err_ref, codes_ref, weights_ref, pair_ref, out_ref, *scratch):
    n_group, _, tokens = codes_ref.shape
    layers, _, _, lat_dev, _ = weights_ref.shape
    n_chips, n_rows, cols = err_ref.shape
    n_near = n_group // layers
    near_lat = n_near * lat_dev
    parts = cols // LANES
    rows, mixed = scratch[:parts], scratch[parts:]
    for i, row in enumerate(rows):
        piece = err_ref[:, :, i * LANES : (i + 1) * LANES].astype(F32)
        row[...] = piece.reshape(n_chips * n_rows, LANES)
    err = []
    for t in range(layers):
        pieces = []
        for first, chip, n in row_blocks(tokens, n_chips, n_near, n_lat):
            start = chip * n_rows + t * n_near + n
            piece = [row[pl.ds(start, n_lat, stride=n_rows), :] for row in rows]
            pieces.append(jnp.concatenate(piece, axis=1))
        err.append(jnp.concatenate(pieces, axis=0).astype(BF16))
    dec_rows = layers * lat_dev
    grad_rows = lat_dev * LANES // cols
    for s in range(layers):
        mine = slice(s * n_near, (s + 1) * n_near)
        codes = codes_ref[mine, :lat_dev].reshape(near_lat, tokens)
        total = jnp.zeros((near_lat, tokens), F32)
        for t in range(layers):
            if t < s:
                row = jnp.zeros((near_lat, cols), F32)
            else:
                row = dot(codes, err[t], 1, 0)
                near = weights_ref[s, t]
                total = total + dot(near.reshape(near_lat, cols), err[t], 1, 1)
            for i, part in enumerate(mixed):
                piece = row[:, i * LANES : (i + 1) * LANES]
                part[pl.ds(t, near_lat, stride=layers), :] = piece
        for i, part in enumerate(mixed):
            piece = part[...].reshape(n_near, dec_rows, LANES).astype(BF16)
            out_ref[mine, i, 0:dec_rows] = piece
        total = total.reshape(n_near, parts, grad_rows, tokens).astype(BF16)
        out_ref[mine, :, dec_rows : dec_rows + grad_rows] = total
    for g in range(n_group):
        for i in range(parts):
            lanes = slice(i * LANES, (i + 1) * LANES)
            high = jnp.broadcast_to(pair_ref[0, g : g + 1, lanes], (8, LANES))
            low = jnp.broadcast_to(pair_ref[1, g : g + 1, lanes], (8, LANES))
            first = lax.broadcasted_iota(jnp.int32, (8, LANES), 0) == 0
            out_ref[g, i, dec_rows + grad_rows :] = jnp.where(first, high, low).astype(BF16)


def finish(
    layers, arrived_ref, tiles_ref, features_ref, active_ref, enc_ref, errors_ref, dec_ref
):
    n_group, parts, n_rows, _ = arrived_ref.shape
    lat_dev, tokens = active_ref.shape
    grad_rows = lat_dev // parts
    dec_rows = n_rows - grad_rows - 8
    n_near = n_group // layers

    def column(g, i):
        return ((g % n_near * layers + g // n_near) * parts + i) * LANES

    for g in range(n_group):
        for i in range(parts):
            first = column(g, i)
            dec_ref[:, :, first : first + LANES] = tiles_ref[g, i, 0:lat_dev]
    halves = []
    for i in range(parts):
        total = arrived_ref[0, i, dec_rows : dec_rows + grad_rows].astype(F32)
        for g in range(1, n_group):
            total = total + arrived_ref[g, i, dec_rows : dec_rows + grad_rows].astype(F32)
        halves.append(total)
    pre_grad = (jnp.concatenate(halves, axis=0) * active_ref[...]).astype(BF16)
    blocks, _, depth = features_ref.shape
    for j in range(blocks):
        enc_ref[:, j * depth : (j + 1) * depth] = dot(pre_grad, features_ref[j], 1, 0).astype(BF16)
    for g in range(n_group):
        for i in range(parts):
            pair = arrived_ref[g, i, dec_rows + grad_rows :].astype(F32)
            errors_ref[:, column(g, i) : column(g, i) + LANES] = pair[0:1] + pair[1:2]


def shift(value, axis, by):
    count = lax.axis_size(axis)
    return lax.ppermute(value, axis, [(i, (i + by) % count) for i in range(count)])


def per_device(inputs, targets, top_index, enc_weight, dec_weight):
    layers, tokens, depth = inputs.shape
    lat_dev = enc_weight.shape[1]
    width = dec_weight.shape[2]
    n_group, n_chips, n_lat = lax.axis_size(GROUP), lax.axis_size(CHIPS), lax.axis_size(LAT)
    n_near = n_group // layers
    cols = width // n_group
    half = width // n_near
    dec_rows = layers * lat_dev
    grad_rows = lat_dev * LANES // cols
    parts = cols // LANES
    x, core = lax.axis_index("x"), lax.axis_index("core")
    lat_first = lax.axis_index(("zp", "zn", "core", "zh", "y")) * lat_dev
    place = jnp.stack([x, lat_first]).astype(jnp.int32)

    n_y = lax.axis_size("y")
    pairs = [[zp * 2 + 0, (1 - zp) * 2 + 1] for zp in range(2)]
    groups = [[i * n_y + y for i in pair for y in range(n_y)] for pair in pairs]
    own = lax.dynamic_slice_in_dim(inputs, x, 1, 0)
    own = jnp.broadcast_to(own, (n_lat, tokens, depth))
    features = lax.all_to_all(own, NEAR_HALVES, 0, 0, tiled=True, axis_index_groups=groups)

    came = shift(dec_weight, "core", 1)
    kept, came = lax.optimization_barrier((dec_weight, came))
    kept = lax.dynamic_slice_in_dim(kept, core * half, half, 2)
    came = lax.dynamic_slice_in_dim(came, core * half, half, 2)
    mine = jnp.where(core == 0, jnp.stack([kept, came]), jnp.stack([came, kept]))
    mine = mine.reshape(n_near, lat_dev, layers, layers, cols).transpose(3, 2, 0, 1, 4)
    active = call(
        find_active,
        shape((lat_dev, tokens), F32),
        place,
        top_index.transpose(0, 2, 1),
        scalars=1,
    )
    codes = call(
        functools.partial(encode, n_near),
        shape((n_group, lat_dev + 8, tokens)),
        features,
        targets,
        enc_weight.T,
        active,
    )
    pieces = []
    for d in range(layers):
        pieces.append(lax.dynamic_index_in_dim(mine, (x + d) % layers, 0, keepdims=False))

    order = sorted(range(layers), key=lambda d: min(d, layers - d))
    for d in order[1:]:
        pieces[d] = shift(pieces[d], "x", d)
    arrived_codes = exchange(codes, GROUP)
    weights = call(
        functools.partial(arrange, order),
        shape((layers, layers, n_near, lat_dev, cols)),
        place,
        codes,
        *[pieces[d] for d in order],
        scalars=1,
    )

    partial = call(
        functools.partial(decode, n_lat),
        shape((n_chips, n_group, cols)),
        arrived_codes,
        weights,
        scratch=[pltpu.VMEM((n_chips * n_group, LANES), F32)] * (cols // LANES),
    )
    partial = exchange(partial, CHIPS)
    err_b, pair = call(
        sum_rows,
        (shape((n_chips, n_group, cols)), shape((2, n_group, cols), F32)),
        partial,
        arrived_codes,
    )
    err_b = exchange(err_b, CHIPS)
    outgoing = call(
        functools.partial(backward, n_lat),
        shape((n_group, parts, dec_rows + grad_rows + 8, LANES)),
        err_b,
        arrived_codes,
        weights,
        pair,
        scratch=[pltpu.VMEM((n_chips * n_group, LANES), F32)] * (cols // LANES)
        + [pltpu.VMEM((n_near * dec_rows, LANES), F32)] * (cols // LANES),
    )
    arrived = exchange(outgoing, GROUP)
    grad_enc, errors, grad_dec = call(
        functools.partial(finish, layers),
        (shape((lat_dev, width)), shape((1, width), F32), shape((lat_dev, layers, width))),
        arrived,
        arrived.reshape(n_group, parts, -1, layers, LANES),
        features,
        active,
    )
    return errors, grad_enc.T, grad_dec


def solution(mesh):
    fine = Mesh(mesh.devices.reshape(4, 2, 2, 2, 2, 8), AXES)
    in_specs = (
        P(None, None, LAT),
        P(AXES, None),
        P(),
        P(None, AXES),
        P(AXES, None, None),
    )
    out_specs = (P(AXES, None), P(None, AXES), P(AXES, None, None))
    return jax.shard_map(
        per_device, mesh=fine, in_specs=in_specs, out_specs=out_specs, check_vma=False
    )
```

```python
import functools

import jax
import jax.numpy as jnp
from jax import lax
from jax.experimental import pallas as pl
from jax.experimental.pallas import tpu as pltpu
from jax.sharding import Mesh
from jax.sharding import PartitionSpec as P

AXES = ("x", "zp", "zn", "core", "zh", "y")
GROUP = ("x", "core")
CHIPS = ("zp", "zn", "zh", "y")
LAT = ("zh", "y")
NEAR_HALVES = ("zp", "zh", "y")
F32 = jnp.float32
BF16 = jnp.bfloat16
LANES = 128


def exchange(value, axes):
    return lax.all_to_all(value, axes, 0, 0, tiled=True)


def dot(a, b, dim_a, dim_b):
    return lax.dot_general(a, b, (((dim_a,), (dim_b,)), ((), ())), preferred_element_type=F32)


def call(body, out_shape, *args, scalars=0, scratch=()):
    specs = [pl.BlockSpec(memory_space=pltpu.SMEM)] * scalars
    specs += [pl.BlockSpec(memory_space=pltpu.VMEM)] * (len(args) - scalars)
    return pl.pallas_call(
        body,
        out_shape=out_shape,
        in_specs=specs,
        out_specs=jax.tree.map(lambda _: pl.BlockSpec(memory_space=pltpu.VMEM), out_shape),
        scratch_shapes=list(scratch),
        compiler_params=pltpu.CompilerParams(vmem_limit_bytes=40 * 1024 * 1024),
    )(*args)


def shape(dims, dtype=BF16):
    return jax.ShapeDtypeStruct(dims, dtype)


def find_active(place, chosen_ref, active_ref):
    ids = place[1] + lax.broadcasted_iota(jnp.int32, active_ref.shape, 0)
    chosen = chosen_ref[place[0]]
    active = jnp.zeros(active_ref.shape, F32)
    for k in range(chosen.shape[0]):
        active = jnp.where(chosen[k : k + 1] == ids, 1.0, active)
    active_ref[...] = active


def encode(n_near, features_ref, target_ref, enc_ref, active_ref, codes_ref):
    parts, tokens, depth = features_ref.shape
    lat_dev = enc_ref.shape[0]
    total = jnp.zeros((lat_dev, tokens), F32)
    for j in range(0, parts, 2):
        pair = jnp.concatenate([features_ref[j], features_ref[j + 1]], axis=1)
        total = total + dot(enc_ref[:, j * depth : (j + 2) * depth], pair, 1, 1)
    codes = (total * active_ref[...]).astype(BF16)
    n_group = codes_ref.shape[0]
    cols = target_ref.shape[1] // n_group
    for g in range(n_group):
        codes_ref[g, :lat_dev] = codes
        first = (g % n_near * (n_group // n_near) + g // n_near) * cols
        target = target_ref[:, first : first + cols].astype(F32)
        pair = [target[:, i : i + LANES] for i in range(0, cols, LANES)]
        rows = jnp.concatenate(pair + [jnp.zeros((8 - len(pair), LANES), F32)], axis=0)
        codes_ref[g, lat_dev:] = rows.astype(BF16)


def row_blocks(tokens, n_chips, n_near, n_lat):
    for p in range(n_chips // n_lat):
        for n in range(n_near):
            yield (p * n_near + n) * n_lat, p * n_lat, n


def arrange(order, place, after, p0, p1, p2, p3, weights_ref):
    del after
    layers = weights_ref.shape[0]
    for d, piece in zip(order, (p0, p1, p2, p3)):
        weights_ref[lax.rem(place[0] + layers - d, layers)] = piece[...]


def decode(n_lat, codes_ref, weights_ref, out_ref, *rows):
    n_group, _, tokens = codes_ref.shape
    n_chips, n_rows, cols = out_ref.shape
    layers, _, _, lat_dev, _ = weights_ref.shape
    n_near = n_group // layers
    flipped = []
    for s in range(layers):
        mine = codes_ref[s * n_near : (s + 1) * n_near, :lat_dev].reshape(-1, tokens)
        flipped.append(mine.T)
    for t in range(layers):
        total = jnp.zeros((tokens, cols), F32)
        for s in range(t + 1):
            near = weights_ref[s, t].reshape(n_near * lat_dev, cols)
            total = total + dot(flipped[s], near, 1, 0)
        for first, chip, n in row_blocks(tokens, n_chips, n_near, n_lat):
            start = chip * n_rows + t * n_near + n
            for i, row in enumerate(rows):
                piece = total[first : first + n_lat, i * LANES : (i + 1) * LANES]
                row[pl.ds(start, n_lat, stride=n_rows), :] = piece
    for i, row in enumerate(rows):
        piece = row[...].reshape(n_chips, n_rows, LANES).astype(BF16)
        out_ref[:, :, i * LANES : (i + 1) * LANES] = piece


def sum_rows(partial_ref, codes_ref, err_ref, pair_ref):
    n_chips, n_rows, cols = partial_ref.shape
    total = partial_ref[0].astype(F32)
    for c in range(1, n_chips):
        total = total + partial_ref[c].astype(F32)
    first = codes_ref.shape[1] - 8
    target = []
    for g in range(n_rows):
        rows = codes_ref[g, first:].astype(F32)
        target.append(jnp.concatenate([rows[i : i + 1] for i in range(cols // LANES)], axis=1))
    target = jnp.concatenate(target, axis=0)
    errors = total - target
    err_b = errors.astype(BF16)
    high = err_b.astype(F32)
    pair_ref[0] = high
    pair_ref[1] = errors - high
    for c in range(n_chips):
        err_ref[c] = err_b


def backward(n_lat, err_ref, codes_ref, weights_ref, pair_ref, out_ref, *scratch):
    n_group, _, tokens = codes_ref.shape
    layers, _, _, lat_dev, _ = weights_ref.shape
    n_chips, n_rows, cols = err_ref.shape
    n_near = n_group // layers
    near_lat = n_near * lat_dev
    parts = cols // LANES
    rows, mixed = scratch[:parts], scratch[parts:]
    for i, row in enumerate(rows):
        piece = err_ref[:, :, i * LANES : (i + 1) * LANES].astype(F32)
        row[...] = piece.reshape(n_chips * n_rows, LANES)
    err = []
    for t in range(layers):
        pieces = []
        for first, chip, n in row_blocks(tokens, n_chips, n_near, n_lat):
            start = chip * n_rows + t * n_near + n
            piece = [row[pl.ds(start, n_lat, stride=n_rows), :] for row in rows]
            pieces.append(jnp.concatenate(piece, axis=1))
        err.append(jnp.concatenate(pieces, axis=0).astype(BF16))
    dec_rows = layers * lat_dev
    for s in range(layers):
        mine = slice(s * n_near, (s + 1) * n_near)
        codes = codes_ref[mine, :lat_dev].reshape(near_lat, tokens)
        total = jnp.zeros((near_lat, tokens), F32)
        for t in range(layers):
            if t < s:
                row = jnp.zeros((near_lat, cols), F32)
            else:
                row = dot(codes, err[t], 1, 0)
                near = weights_ref[s, t]
                total = total + dot(near.reshape(near_lat, cols), err[t], 1, 1)
            for i, part in enumerate(mixed):
                piece = row[:, i * LANES : (i + 1) * LANES]
                part[pl.ds(t, near_lat, stride=layers), :] = piece
        for i, part in enumerate(mixed):
            piece = part[...].reshape(n_near, dec_rows, LANES).astype(BF16)
            out_ref[mine, i * dec_rows : (i + 1) * dec_rows] = piece
        total = total.reshape(n_near, lat_dev, tokens).astype(BF16)
        out_ref[mine, parts * dec_rows : parts * dec_rows + lat_dev] = total
    for g in range(n_group):
        pair = [
            pair_ref[k, g : g + 1, i * LANES : (i + 1) * LANES]
            for k in range(2)
            for i in range(parts)
        ]
        tile = jnp.concatenate(pair + [jnp.zeros((8 - len(pair), LANES), F32)], axis=0)
        out_ref[g, parts * dec_rows + lat_dev :] = tile.astype(BF16)


def finish(
    layers, arrived_ref, tiles_ref, features_ref, active_ref, enc_ref, errors_ref, dec_ref
):
    n_group = arrived_ref.shape[0]
    lat_dev = active_ref.shape[0]
    parts = errors_ref.shape[1] // (n_group * LANES)
    first_grad = parts * layers * lat_dev
    grads = slice(first_grad, first_grad + lat_dev)
    n_near = n_group // layers

    def column(g, i):
        return ((g % n_near * layers + g // n_near) * parts + i) * LANES

    for g in range(n_group):
        for i in range(parts):
            first = column(g, i)
            dec_ref[:, :, first : first + LANES] = tiles_ref[g, i * lat_dev : (i + 1) * lat_dev]
    total = arrived_ref[0, grads].astype(F32)
    for g in range(1, n_group):
        total = total + arrived_ref[g, grads].astype(F32)
    pre_grad = (total * active_ref[...]).astype(BF16)
    blocks, _, depth = features_ref.shape
    for j in range(0, blocks, 2):
        pair = jnp.concatenate([features_ref[j], features_ref[j + 1]], axis=1)
        enc_ref[:, j * depth : (j + 2) * depth] = dot(pre_grad, pair, 1, 0).astype(BF16)
    for g in range(n_group):
        pair = arrived_ref[g, first_grad + lat_dev :].astype(F32)
        for i in range(parts):
            row = pair[i : i + 1] + pair[parts + i : parts + i + 1]
            errors_ref[:, column(g, i) : column(g, i) + LANES] = row


def shift(value, axis, by):
    count = lax.axis_size(axis)
    return lax.ppermute(value, axis, [(i, (i + by) % count) for i in range(count)])


def per_device(inputs, targets, top_index, enc_weight, dec_weight):
    layers, tokens, depth = inputs.shape
    lat_dev = enc_weight.shape[1]
    width = dec_weight.shape[2]
    n_group, n_chips, n_lat = lax.axis_size(GROUP), lax.axis_size(CHIPS), lax.axis_size(LAT)
    n_near = n_group // layers
    cols = width // n_group
    half = width // n_near
    dec_rows = layers * lat_dev
    parts = cols // LANES
    x, core = lax.axis_index("x"), lax.axis_index("core")
    lat_first = lax.axis_index(("zp", "zn", "core", "zh", "y")) * lat_dev
    place = jnp.stack([x, lat_first]).astype(jnp.int32)

    n_y = lax.axis_size("y")
    pairs = [[zp * 2 + 0, (1 - zp) * 2 + 1] for zp in range(2)]
    groups = [[i * n_y + y for i in pair for y in range(n_y)] for pair in pairs]
    own = lax.dynamic_slice_in_dim(inputs, x, 1, 0)
    own = jnp.broadcast_to(own, (n_lat, tokens, depth))
    features = lax.all_to_all(own, NEAR_HALVES, 0, 0, tiled=True, axis_index_groups=groups)

    came = shift(dec_weight, "core", 1)
    kept, came = lax.optimization_barrier((dec_weight, came))
    kept = lax.dynamic_slice_in_dim(kept, core * half, half, 2)
    came = lax.dynamic_slice_in_dim(came, core * half, half, 2)
    mine = jnp.where(core == 0, jnp.stack([kept, came]), jnp.stack([came, kept]))
    mine = mine.reshape(n_near, lat_dev, layers, layers, cols).transpose(3, 2, 0, 1, 4)
    active = call(
        find_active,
        shape((lat_dev, tokens), F32),
        place,
        top_index.transpose(0, 2, 1),
        scalars=1,
    )
    codes = call(
        functools.partial(encode, n_near),
        shape((n_group, lat_dev + 8, tokens)),
        features,
        targets,
        enc_weight.T,
        active,
    )
    pieces = []
    for d in range(layers):
        pieces.append(lax.dynamic_index_in_dim(mine, (x + d) % layers, 0, keepdims=False))

    order = sorted(range(layers), key=lambda d: min(d, layers - d))
    for d in order[1:]:
        pieces[d] = shift(pieces[d], "x", d)
    arrived_codes = exchange(codes, GROUP)
    weights = call(
        functools.partial(arrange, order),
        shape((layers, layers, n_near, lat_dev, cols)),
        place,
        codes,
        *[pieces[d] for d in order],
        scalars=1,
    )

    partial = call(
        functools.partial(decode, n_lat),
        shape((n_chips, n_group, cols)),
        arrived_codes,
        weights,
        scratch=[pltpu.VMEM((n_chips * n_group, LANES), F32)] * (cols // LANES),
    )
    partial = exchange(partial, CHIPS)
    err_b, pair = call(
        sum_rows,
        (shape((n_chips, n_group, cols)), shape((2, n_group, cols), F32)),
        partial,
        arrived_codes,
    )
    err_b = exchange(err_b, CHIPS)
    outgoing = call(
        functools.partial(backward, n_lat),
        shape((n_group, parts * dec_rows + lat_dev + 8, LANES)),
        err_b,
        arrived_codes,
        weights,
        pair,
        scratch=[pltpu.VMEM((n_chips * n_group, LANES), F32)] * (cols // LANES)
        + [pltpu.VMEM((n_near * dec_rows, LANES), F32)] * (cols // LANES),
    )
    arrived = exchange(outgoing, GROUP)
    grad_enc, errors, grad_dec = call(
        functools.partial(finish, layers),
        (shape((lat_dev, width)), shape((1, width), F32), shape((lat_dev, layers, width))),
        arrived,
        arrived.reshape(n_group, -1, layers, LANES),
        features,
        active,
    )
    return errors, grad_enc.T, grad_dec


def solution(mesh):
    fine = Mesh(mesh.devices.reshape(4, 2, 2, 2, 2, 8), AXES)
    in_specs = (
        P(None, None, LAT),
        P(AXES, None),
        P(),
        P(None, AXES),
        P(AXES, None, None),
    )
    out_specs = (P(AXES, None), P(None, AXES), P(AXES, None, None))
    return jax.shard_map(
        per_device, mesh=fine, in_specs=in_specs, out_specs=out_specs, check_vma=False
    )
```

```python
import functools

import jax
import jax.numpy as jnp
from jax import lax
from jax.experimental import pallas as pl
from jax.experimental.pallas import tpu as pltpu
from jax.sharding import Mesh
from jax.sharding import PartitionSpec as P

AXES = ("x", "zp", "zn", "core", "zh", "y")
GROUP = ("x", "core")
CHIPS = ("zp", "zn", "zh", "y")
LAT = ("zh", "y")
NEAR_HALVES = ("zp", "zh", "y")
F32 = jnp.float32
BF16 = jnp.bfloat16
LANES = 128


def exchange(value, axes):
    return lax.all_to_all(value, axes, 0, 0, tiled=True)


def dot(a, b, dim_a, dim_b):
    return lax.dot_general(a, b, (((dim_a,), (dim_b,)), ((), ())), preferred_element_type=F32)


def call(body, out_shape, *args, scalars=0, scratch=()):
    specs = [pl.BlockSpec(memory_space=pltpu.SMEM)] * scalars
    specs += [pl.BlockSpec(memory_space=pltpu.VMEM)] * (len(args) - scalars)
    return pl.pallas_call(
        body,
        out_shape=out_shape,
        in_specs=specs,
        out_specs=jax.tree.map(lambda _: pl.BlockSpec(memory_space=pltpu.VMEM), out_shape),
        scratch_shapes=list(scratch),
        compiler_params=pltpu.CompilerParams(vmem_limit_bytes=40 * 1024 * 1024),
    )(*args)


def shape(dims, dtype=BF16):
    return jax.ShapeDtypeStruct(dims, dtype)


def find_active(place, chosen_ref, active_ref):
    ids = place[1] + lax.broadcasted_iota(jnp.int32, active_ref.shape, 0)
    chosen = chosen_ref[place[0]]
    active = jnp.zeros(active_ref.shape, F32)
    for k in range(chosen.shape[0]):
        active = jnp.where(chosen[k : k + 1] == ids, 1.0, active)
    active_ref[...] = active


def encode(n_near, features_ref, target_ref, enc_ref, active_ref, codes_ref):
    parts, tokens, depth = features_ref.shape
    lat_dev = enc_ref.shape[0]
    total = jnp.zeros((lat_dev, tokens), F32)
    for j in range(0, parts, 4):
        some = jnp.concatenate([features_ref[j + i] for i in range(4)], axis=1)
        total = total + dot(enc_ref[:, j * depth : (j + 4) * depth], some, 1, 1)
    codes = (total * active_ref[...]).astype(BF16)
    n_group = codes_ref.shape[0]
    cols = target_ref.shape[1] // n_group
    for g in range(n_group):
        codes_ref[g, :lat_dev] = codes
        first = (g % n_near * (n_group // n_near) + g // n_near) * cols
        target = target_ref[:, first : first + cols].astype(F32)
        pair = [target[:, i : i + LANES] for i in range(0, cols, LANES)]
        rows = jnp.concatenate(pair + [jnp.zeros((8 - len(pair), LANES), F32)], axis=0)
        codes_ref[g, lat_dev:] = rows.astype(BF16)


def row_blocks(tokens, n_chips, n_near, n_lat):
    for p in range(n_chips // n_lat):
        for n in range(n_near):
            yield (p * n_near + n) * n_lat, p * n_lat, n


def arrange(order, place, after, p0, p1, p2, p3, weights_ref):
    del after
    layers = weights_ref.shape[0]
    for d, piece in zip(order, (p0, p1, p2, p3)):
        weights_ref[lax.rem(place[0] + layers - d, layers)] = piece[...]


def decode(n_lat, codes_ref, weights_ref, out_ref, *rows):
    n_group, _, tokens = codes_ref.shape
    n_chips, n_rows, cols = out_ref.shape
    layers, _, _, lat_dev, _ = weights_ref.shape
    n_near = n_group // layers
    flipped = []
    for s in range(layers):
        mine = codes_ref[s * n_near : (s + 1) * n_near, :lat_dev].reshape(-1, tokens)
        flipped.append(mine.T)
    for t in range(layers):
        total = jnp.zeros((tokens, cols), F32)
        for s in range(t + 1):
            near = weights_ref[s, t].reshape(n_near * lat_dev, cols)
            total = total + dot(flipped[s], near, 1, 0)
        for first, chip, n in row_blocks(tokens, n_chips, n_near, n_lat):
            start = chip * n_rows + t * n_near + n
            for i, row in enumerate(rows):
                piece = total[first : first + n_lat, i * LANES : (i + 1) * LANES]
                row[pl.ds(start, n_lat, stride=n_rows), :] = piece
    for i, row in enumerate(rows):
        piece = row[...].reshape(n_chips, n_rows, LANES).astype(BF16)
        out_ref[:, :, i * LANES : (i + 1) * LANES] = piece


def sum_rows(partial_ref, codes_ref, err_ref, pair_ref):
    n_chips, n_rows, cols = partial_ref.shape
    total = partial_ref[0].astype(F32)
    for c in range(1, n_chips):
        total = total + partial_ref[c].astype(F32)
    first = codes_ref.shape[1] - 8
    target = []
    for g in range(n_rows):
        rows = codes_ref[g, first:].astype(F32)
        target.append(jnp.concatenate([rows[i : i + 1] for i in range(cols // LANES)], axis=1))
    target = jnp.concatenate(target, axis=0)
    errors = total - target
    err_b = errors.astype(BF16)
    high = err_b.astype(F32)
    pair_ref[0] = high
    pair_ref[1] = errors - high
    for c in range(n_chips):
        err_ref[c] = err_b


def backward(n_lat, err_ref, codes_ref, weights_ref, pair_ref, out_ref, *scratch):
    n_group, _, tokens = codes_ref.shape
    layers, _, _, lat_dev, _ = weights_ref.shape
    n_chips, n_rows, cols = err_ref.shape
    n_near = n_group // layers
    near_lat = n_near * lat_dev
    parts = cols // LANES
    rows, mixed = scratch[:parts], scratch[parts:]
    for i, row in enumerate(rows):
        piece = err_ref[:, :, i * LANES : (i + 1) * LANES].astype(F32)
        row[...] = piece.reshape(n_chips * n_rows, LANES)
    err = []
    for t in range(layers):
        pieces = []
        for first, chip, n in row_blocks(tokens, n_chips, n_near, n_lat):
            start = chip * n_rows + t * n_near + n
            piece = [row[pl.ds(start, n_lat, stride=n_rows), :] for row in rows]
            pieces.append(jnp.concatenate(piece, axis=1))
        err.append(jnp.concatenate(pieces, axis=0).astype(BF16))
    dec_rows = layers * lat_dev
    for s in range(layers):
        mine = slice(s * n_near, (s + 1) * n_near)
        codes = codes_ref[mine, :lat_dev].reshape(near_lat, tokens)
        total = jnp.zeros((near_lat, tokens), F32)
        for t in range(layers):
            if t < s:
                row = jnp.zeros((near_lat, cols), F32)
            else:
                row = dot(codes, err[t], 1, 0)
                near = weights_ref[s, t]
                total = total + dot(near.reshape(near_lat, cols), err[t], 1, 1)
            for i, part in enumerate(mixed):
                piece = row[:, i * LANES : (i + 1) * LANES]
                part[pl.ds(t, near_lat, stride=layers), :] = piece
        for i, part in enumerate(mixed):
            piece = part[...].reshape(n_near, dec_rows, LANES).astype(BF16)
            out_ref[mine, i * dec_rows : (i + 1) * dec_rows] = piece
        total = total.reshape(n_near, lat_dev, tokens).astype(BF16)
        out_ref[mine, parts * dec_rows : parts * dec_rows + lat_dev] = total
    for g in range(n_group):
        pair = [
            pair_ref[k, g : g + 1, i * LANES : (i + 1) * LANES]
            for k in range(2)
            for i in range(parts)
        ]
        tile = jnp.concatenate(pair + [jnp.zeros((8 - len(pair), LANES), F32)], axis=0)
        out_ref[g, parts * dec_rows + lat_dev :] = tile.astype(BF16)


def finish(
    layers, arrived_ref, tiles_ref, features_ref, active_ref, enc_ref, errors_ref, dec_ref
):
    n_group = arrived_ref.shape[0]
    lat_dev = active_ref.shape[0]
    parts = errors_ref.shape[1] // (n_group * LANES)
    first_grad = parts * layers * lat_dev
    grads = slice(first_grad, first_grad + lat_dev)
    n_near = n_group // layers

    def column(g, i):
        return ((g % n_near * layers + g // n_near) * parts + i) * LANES

    for g in range(n_group):
        for i in range(parts):
            first = column(g, i)
            dec_ref[:, :, first : first + LANES] = tiles_ref[g, i * lat_dev : (i + 1) * lat_dev]
    total = arrived_ref[0, grads].astype(F32)
    for g in range(1, n_group):
        total = total + arrived_ref[g, grads].astype(F32)
    pre_grad = (total * active_ref[...]).astype(BF16)
    blocks, _, depth = features_ref.shape
    for j in range(0, blocks, 4):
        some = jnp.concatenate([features_ref[j + i] for i in range(4)], axis=1)
        enc_ref[:, j * depth : (j + 4) * depth] = dot(pre_grad, some, 1, 0).astype(BF16)
    for g in range(n_group):
        pair = arrived_ref[g, first_grad + lat_dev :].astype(F32)
        for i in range(parts):
            row = pair[i : i + 1] + pair[parts + i : parts + i + 1]
            errors_ref[:, column(g, i) : column(g, i) + LANES] = row


def shift(value, axis, by):
    count = lax.axis_size(axis)
    return lax.ppermute(value, axis, [(i, (i + by) % count) for i in range(count)])


def per_device(inputs, targets, top_index, enc_weight, dec_weight):
    layers, tokens, depth = inputs.shape
    lat_dev = enc_weight.shape[1]
    width = dec_weight.shape[2]
    n_group, n_chips, n_lat = lax.axis_size(GROUP), lax.axis_size(CHIPS), lax.axis_size(LAT)
    n_near = n_group // layers
    cols = width // n_group
    half = width // n_near
    dec_rows = layers * lat_dev
    parts = cols // LANES
    x, core = lax.axis_index("x"), lax.axis_index("core")
    lat_first = lax.axis_index(("zp", "zn", "core", "zh", "y")) * lat_dev
    place = jnp.stack([x, lat_first]).astype(jnp.int32)

    n_y = lax.axis_size("y")
    pairs = [[zp * 2 + 0, (1 - zp) * 2 + 1] for zp in range(2)]
    groups = [[i * n_y + y for i in pair for y in range(n_y)] for pair in pairs]
    own = lax.dynamic_slice_in_dim(inputs, x, 1, 0)
    own = jnp.broadcast_to(own, (n_lat, tokens, depth))
    features = lax.all_to_all(own, NEAR_HALVES, 0, 0, tiled=True, axis_index_groups=groups)

    came = shift(dec_weight, "core", 1)
    kept, came = lax.optimization_barrier((dec_weight, came))
    kept = lax.dynamic_slice_in_dim(kept, core * half, half, 2)
    came = lax.dynamic_slice_in_dim(came, core * half, half, 2)
    mine = jnp.where(core == 0, jnp.stack([kept, came]), jnp.stack([came, kept]))
    mine = mine.reshape(n_near, lat_dev, layers, layers, cols).transpose(3, 2, 0, 1, 4)
    active = call(
        find_active,
        shape((lat_dev, tokens), F32),
        place,
        top_index.transpose(0, 2, 1),
        scalars=1,
    )
    codes = call(
        functools.partial(encode, n_near),
        shape((n_group, lat_dev + 8, tokens)),
        features,
        targets,
        enc_weight.T,
        active,
    )
    pieces = []
    for d in range(layers):
        pieces.append(lax.dynamic_index_in_dim(mine, (x + d) % layers, 0, keepdims=False))

    order = sorted(range(layers), key=lambda d: min(d, layers - d))
    for d in order[1:]:
        pieces[d] = shift(pieces[d], "x", d)
    arrived_codes = exchange(codes, GROUP)
    weights = call(
        functools.partial(arrange, order),
        shape((layers, layers, n_near, lat_dev, cols)),
        place,
        codes,
        *[pieces[d] for d in order],
        scalars=1,
    )

    partial = call(
        functools.partial(decode, n_lat),
        shape((n_chips, n_group, cols)),
        arrived_codes,
        weights,
        scratch=[pltpu.VMEM((n_chips * n_group, LANES), F32)] * (cols // LANES),
    )
    partial = exchange(partial, CHIPS)
    err_b, pair = call(
        sum_rows,
        (shape((n_chips, n_group, cols)), shape((2, n_group, cols), F32)),
        partial,
        arrived_codes,
    )
    err_b = exchange(err_b, CHIPS)
    outgoing = call(
        functools.partial(backward, n_lat),
        shape((n_group, parts * dec_rows + lat_dev + 8, LANES)),
        err_b,
        arrived_codes,
        weights,
        pair,
        scratch=[pltpu.VMEM((n_chips * n_group, LANES), F32)] * (cols // LANES)
        + [pltpu.VMEM((n_near * dec_rows, LANES), F32)] * (cols // LANES),
    )
    arrived = exchange(outgoing, GROUP)
    grad_enc, errors, grad_dec = call(
        functools.partial(finish, layers),
        (shape((lat_dev, width)), shape((1, width), F32), shape((lat_dev, layers, width))),
        arrived,
        arrived.reshape(n_group, -1, layers, LANES),
        features,
        active,
    )
    return errors, grad_enc.T, grad_dec


def solution(mesh):
    fine = Mesh(mesh.devices.reshape(4, 2, 2, 2, 2, 8), AXES)
    in_specs = (
        P(None, None, LAT),
        P(AXES, None),
        P(),
        P(None, AXES),
        P(AXES, None, None),
    )
    out_specs = (P(AXES, None), P(None, AXES), P(AXES, None, None))
    return jax.shard_map(
        per_device, mesh=fine, in_specs=in_specs, out_specs=out_specs, check_vma=False
    )
```

```python
import functools

import jax
import jax.numpy as jnp
from jax import lax
from jax.experimental import pallas as pl
from jax.experimental.pallas import tpu as pltpu
from jax.sharding import Mesh
from jax.sharding import PartitionSpec as P

AXES = ("x", "zp", "zn", "core", "zh", "y")
GROUP = ("x", "core")
CHIPS = ("zp", "zn", "zh", "y")
LAT = ("zh", "y")
NEAR_HALVES = ("zp", "zh", "y")
F32 = jnp.float32
BF16 = jnp.bfloat16
LANES = 128


def exchange(value, axes):
    return lax.all_to_all(value, axes, 0, 0, tiled=True)


def dot(a, b, dim_a, dim_b):
    return lax.dot_general(a, b, (((dim_a,), (dim_b,)), ((), ())), preferred_element_type=F32)


def call(body, out_shape, *args, scalars=0, scratch=()):
    specs = [pl.BlockSpec(memory_space=pltpu.SMEM)] * scalars
    specs += [pl.BlockSpec(memory_space=pltpu.VMEM)] * (len(args) - scalars)
    return pl.pallas_call(
        body,
        out_shape=out_shape,
        in_specs=specs,
        out_specs=jax.tree.map(lambda _: pl.BlockSpec(memory_space=pltpu.VMEM), out_shape),
        scratch_shapes=list(scratch),
        compiler_params=pltpu.CompilerParams(vmem_limit_bytes=40 * 1024 * 1024),
    )(*args)


def shape(dims, dtype=BF16):
    return jax.ShapeDtypeStruct(dims, dtype)


def find_active(place, chosen_ref, active_ref):
    ids = place[1] + lax.broadcasted_iota(jnp.int32, active_ref.shape, 0)
    chosen = chosen_ref[place[0]]
    active = jnp.zeros(active_ref.shape, F32)
    for k in range(chosen.shape[0]):
        active = jnp.where(chosen[k : k + 1] == ids, 1.0, active)
    active_ref[...] = active


def encode(n_near, features_ref, target_ref, enc_ref, active_ref, codes_ref):
    parts, tokens, depth = features_ref.shape
    lat_dev = enc_ref.shape[0]
    total = jnp.zeros((lat_dev, tokens), F32)
    for j in range(0, parts, 2):
        pair = jnp.concatenate([features_ref[j], features_ref[j + 1]], axis=1)
        total = total + dot(enc_ref[:, j * depth : (j + 2) * depth], pair, 1, 1)
    codes = (total * active_ref[...]).astype(BF16)
    n_group = codes_ref.shape[0]
    cols = target_ref.shape[1] // n_group
    for g in range(n_group):
        codes_ref[g, :lat_dev] = codes
        first = (g % n_near * (n_group // n_near) + g // n_near) * cols
        target = target_ref[:, first : first + cols].astype(F32)
        pair = [target[:, i : i + LANES] for i in range(0, cols, LANES)]
        rows = jnp.concatenate(pair + [jnp.zeros((8 - len(pair), LANES), F32)], axis=0)
        codes_ref[g, lat_dev:] = rows.astype(BF16)


def row_blocks(tokens, n_chips, n_near, n_lat):
    for p in range(n_chips // n_lat):
        for n in range(n_near):
            yield (p * n_near + n) * n_lat, p * n_lat, n


def arrange(order, place, after, p0, p1, p2, p3, weights_ref):
    del after
    layers = weights_ref.shape[0]
    for d, piece in zip(order, (p0, p1, p2, p3)):
        weights_ref[lax.rem(place[0] + layers - d, layers)] = piece[...]


def decode(n_lat, codes_ref, weights_ref, out_ref, *rows):
    n_group, _, tokens = codes_ref.shape
    n_chips, n_rows, cols = out_ref.shape
    layers, _, _, lat_dev, _ = weights_ref.shape
    n_near = n_group // layers
    flipped = []
    for s in range(layers):
        mine = codes_ref[s * n_near : (s + 1) * n_near, :lat_dev].reshape(-1, tokens)
        flipped.append(mine.T)
    for t in range(layers):
        total = jnp.zeros((tokens, cols), F32)
        for s in range(t + 1):
            near = weights_ref[s, t].reshape(n_near * lat_dev, cols)
            total = total + dot(flipped[s], near, 1, 0)
        for first, chip, n in row_blocks(tokens, n_chips, n_near, n_lat):
            start = chip * n_rows + t * n_near + n
            for i, row in enumerate(rows):
                piece = total[first : first + n_lat, i * LANES : (i + 1) * LANES]
                row[pl.ds(start, n_lat, stride=n_rows), :] = piece
    for i, row in enumerate(rows):
        piece = row[...].reshape(n_chips, n_rows, LANES).astype(BF16)
        out_ref[:, :, i * LANES : (i + 1) * LANES] = piece


def sum_rows(partial_ref, codes_ref, err_ref, pair_ref):
    n_chips, n_rows, cols = partial_ref.shape
    total = partial_ref[0].astype(F32)
    for c in range(1, n_chips):
        total = total + partial_ref[c].astype(F32)
    first = codes_ref.shape[1] - 8
    target = []
    for g in range(n_rows):
        rows = codes_ref[g, first:].astype(F32)
        target.append(jnp.concatenate([rows[i : i + 1] for i in range(cols // LANES)], axis=1))
    target = jnp.concatenate(target, axis=0)
    errors = total - target
    err_b = errors.astype(BF16)
    high = err_b.astype(F32)
    pair_ref[0] = high
    pair_ref[1] = errors - high
    for c in range(n_chips):
        err_ref[c] = err_b


def backward(n_lat, err_ref, codes_ref, weights_ref, pair_ref, out_ref, *scratch):
    n_group, _, tokens = codes_ref.shape
    layers, _, _, lat_dev, _ = weights_ref.shape
    n_chips, n_rows, cols = err_ref.shape
    n_near = n_group // layers
    near_lat = n_near * lat_dev
    parts = cols // LANES
    rows, mixed = scratch[:parts], scratch[parts:]
    for i, row in enumerate(rows):
        piece = err_ref[:, :, i * LANES : (i + 1) * LANES].astype(F32)
        row[...] = piece.reshape(n_chips * n_rows, LANES)
    err = []
    for t in range(layers):
        pieces = []
        for first, chip, n in row_blocks(tokens, n_chips, n_near, n_lat):
            start = chip * n_rows + t * n_near + n
            piece = [row[pl.ds(start, n_lat, stride=n_rows), :] for row in rows]
            pieces.append(jnp.concatenate(piece, axis=1))
        err.append(jnp.concatenate(pieces, axis=0).astype(BF16))
    dec_rows = layers * lat_dev
    for s in range(layers):
        mine = slice(s * n_near, (s + 1) * n_near)
        codes = codes_ref[mine, :lat_dev].reshape(near_lat, tokens)
        total = jnp.zeros((near_lat, tokens), F32)
        for t in range(layers):
            if t < s:
                row = jnp.zeros((near_lat, cols), F32)
            else:
                row = dot(codes, err[t], 1, 0)
                near = weights_ref[s, t]
                total = total + dot(near.reshape(near_lat, cols), err[t], 1, 1)
            for i, part in enumerate(mixed):
                piece = row[:, i * LANES : (i + 1) * LANES]
                part[pl.ds(t, near_lat, stride=layers), :] = piece
        for i, part in enumerate(mixed):
            piece = part[...].reshape(n_near, dec_rows, LANES).astype(BF16)
            out_ref[mine, i * dec_rows : (i + 1) * dec_rows] = piece
        total = total.reshape(n_near, lat_dev, tokens).astype(BF16)
        out_ref[mine, parts * dec_rows : parts * dec_rows + lat_dev] = total
    for g in range(n_group):
        pair = [
            pair_ref[k, g : g + 1, i * LANES : (i + 1) * LANES]
            for k in range(2)
            for i in range(parts)
        ]
        tile = jnp.concatenate(pair + [jnp.zeros((8 - len(pair), LANES), F32)], axis=0)
        out_ref[g, parts * dec_rows + lat_dev :] = tile.astype(BF16)


def finish(
    layers, arrived_ref, tiles_ref, features_ref, active_ref, enc_ref, errors_ref, dec_ref
):
    n_group = arrived_ref.shape[0]
    lat_dev = active_ref.shape[0]
    parts = errors_ref.shape[1] // (n_group * LANES)
    first_grad = parts * layers * lat_dev
    grads = slice(first_grad, first_grad + lat_dev)
    n_near = n_group // layers

    def column(g, i):
        return ((g % n_near * layers + g // n_near) * parts + i) * LANES

    for g in range(n_group):
        for i in range(parts):
            first = column(g, i)
            dec_ref[:, :, first : first + LANES] = tiles_ref[g, i * lat_dev : (i + 1) * lat_dev]
    total = arrived_ref[0, grads].astype(F32)
    for g in range(1, n_group):
        total = total + arrived_ref[g, grads].astype(F32)
    pre_grad = (total * active_ref[...]).astype(BF16)
    blocks, _, depth = features_ref.shape
    for j in range(0, blocks, 2):
        pair = jnp.concatenate([features_ref[j], features_ref[j + 1]], axis=1)
        enc_ref[:, j * depth : (j + 2) * depth] = dot(pre_grad, pair, 1, 0).astype(BF16)
    for g in range(n_group):
        pair = arrived_ref[g, first_grad + lat_dev :].astype(F32)
        for i in range(parts):
            row = pair[i : i + 1] + pair[parts + i : parts + i + 1]
            errors_ref[:, column(g, i) : column(g, i) + LANES] = row


def shift(value, axis, by):
    count = lax.axis_size(axis)
    return lax.ppermute(value, axis, [(i, (i + by) % count) for i in range(count)])


def per_device(inputs, targets, top_index, enc_weight, dec_weight):
    layers, tokens, depth = inputs.shape
    lat_dev = enc_weight.shape[1]
    width = dec_weight.shape[2]
    n_group, n_chips, n_lat = lax.axis_size(GROUP), lax.axis_size(CHIPS), lax.axis_size(LAT)
    n_near = n_group // layers
    cols = width // n_group
    half = width // n_near
    dec_rows = layers * lat_dev
    parts = cols // LANES
    x, core = lax.axis_index("x"), lax.axis_index("core")
    lat_first = lax.axis_index(("zp", "zn", "core", "zh", "y")) * lat_dev
    place = jnp.stack([x, lat_first]).astype(jnp.int32)

    n_y = lax.axis_size("y")
    pairs = [[zp * 2 + 0, (1 - zp) * 2 + 1] for zp in range(2)]
    groups = [[i * n_y + y for i in pair for y in range(n_y)] for pair in pairs]
    own = lax.dynamic_slice_in_dim(inputs, x, 1, 0)
    own = jnp.broadcast_to(own, (n_lat, tokens, depth))
    features = lax.all_to_all(own, NEAR_HALVES, 0, 0, tiled=True, axis_index_groups=groups)

    came = shift(dec_weight, "core", 1)
    kept, came = lax.optimization_barrier((dec_weight, came))
    kept = lax.dynamic_slice_in_dim(kept, core * half, half, 2)
    came = lax.dynamic_slice_in_dim(came, core * half, half, 2)
    mine = jnp.where(core == 0, jnp.stack([kept, came]), jnp.stack([came, kept]))
    mine = mine.reshape(n_near, lat_dev, layers, layers, cols).transpose(3, 2, 0, 1, 4)
    active = call(
        find_active,
        shape((lat_dev, tokens), F32),
        place,
        top_index.transpose(0, 2, 1),
        scalars=1,
    )
    codes = call(
        functools.partial(encode, n_near),
        shape((n_group, lat_dev + 8, tokens)),
        features,
        targets,
        enc_weight.T,
        active,
    )
    pieces = []
    for d in range(layers):
        pieces.append(lax.dynamic_index_in_dim(mine, (x + d) % layers, 0, keepdims=False))

    order = [0] + list(range(layers - 1, 0, -1))
    for d in order[1:]:
        pieces[d] = shift(pieces[d], "x", d)
    arrived_codes = exchange(codes, GROUP)
    weights = call(
        functools.partial(arrange, order),
        shape((layers, layers, n_near, lat_dev, cols)),
        place,
        codes,
        *[pieces[d] for d in order],
        scalars=1,
    )

    partial = call(
        functools.partial(decode, n_lat),
        shape((n_chips, n_group, cols)),
        arrived_codes,
        weights,
        scratch=[pltpu.VMEM((n_chips * n_group, LANES), F32)] * (cols // LANES),
    )
    partial = exchange(partial, CHIPS)
    err_b, pair = call(
        sum_rows,
        (shape((n_chips, n_group, cols)), shape((2, n_group, cols), F32)),
        partial,
        arrived_codes,
    )
    err_b = exchange(err_b, CHIPS)
    outgoing = call(
        functools.partial(backward, n_lat),
        shape((n_group, parts * dec_rows + lat_dev + 8, LANES)),
        err_b,
        arrived_codes,
        weights,
        pair,
        scratch=[pltpu.VMEM((n_chips * n_group, LANES), F32)] * (cols // LANES)
        + [pltpu.VMEM((n_near * dec_rows, LANES), F32)] * (cols // LANES),
    )
    arrived = exchange(outgoing, GROUP)
    grad_enc, errors, grad_dec = call(
        functools.partial(finish, layers),
        (shape((lat_dev, width)), shape((1, width), F32), shape((lat_dev, layers, width))),
        arrived,
        arrived.reshape(n_group, -1, layers, LANES),
        features,
        active,
    )
    return errors, grad_enc.T, grad_dec


def solution(mesh):
    fine = Mesh(mesh.devices.reshape(4, 2, 2, 2, 2, 8), AXES)
    in_specs = (
        P(None, None, LAT),
        P(AXES, None),
        P(),
        P(None, AXES),
        P(AXES, None, None),
    )
    out_specs = (P(AXES, None), P(None, AXES), P(AXES, None, None))
    return jax.shard_map(
        per_device, mesh=fine, in_specs=in_specs, out_specs=out_specs, check_vma=False
    )
```
